256 devices in a mesh: dom: 64 (over y, z, core), feat: 4 (over x).
Axes of the slice: x: 4, y: 4, z: 8, core: 2. Of those that a mesh axis runs over, the one named last changes fastest.
Arguments:
- features: bfloat16 [128, 65536], P('feat', 'dom'), may hold values from -6 to 6
- tile_mask: int32 [1536, 6, 128, 128], P('dom'), may hold values 0 or 1
- tile_cols: int32 [1536, 6], P('dom'), may hold values from 0 to 23, as said below
- replicas: int32 [3, 131072], P(None, 'dom'), may hold values from 0 to 1023, as said below
- degree: int32 [65536], P('dom'), may hold values from 12 to 47
- self_one: bfloat16 [128, 256], replicated, may hold values from -0.5 to 0.5
- neigh_one: bfloat16 [128, 256], replicated, may hold values from -2 to 2
- self_two: bfloat16 [256, 256], replicated, may hold values from -0.375 to 0.375
- neigh_two: bfloat16 [256, 256], replicated, may hold values from -1.5 to 1.5
Outputs:
- embed: bfloat16 [256, 65536], P('feat', 'dom')
The draws below stay inside these ranges and needn't reach their ends.
Inputs may be any that keep to these rules, and one draw needn't show every extreme that they name: replicas[0] never names the mirror's own partition; a partition's mirrors with one master partition have distinct slots 0 to at most 63 and distinct master rows; in every draw some master partition receives exactly 64 mirrors from every other partition. `tile_cols`: the 6 column blocks of one row of blocks are distinct.
All inputs are finite; a program needn't handle non-finite values. No bound on the sum of `tile_mask` on one device may be relied on, other than what follows from the above.
Results may differ from the reference program's by a relative error of at most 0.0027.
The reference program's roundings to bfloat16 on the way count: a program that leaves them out, or rounds other values in their place, can miss the bound.
Values may be sent and summed in bfloat16 or wider, within the bound.
A program may use at most 64 MiB of HBM per device.

```python
import jax
import jax.numpy as jnp
from jax import lax

FIN = 128
HID = 256
MAST = 1024
TILE = 128
K = 6
MIRROR_VERTICES = 2048
ROWS = 3072
TILES = 24
EDGE_PARTITIONS = 64
CAP = 64
NM = 65536


def draw_tile_cols(key, part):
    keys = jax.random.split(jax.random.fold_in(key, 11), EDGE_PARTITIONS * TILES)
    chosen = jax.vmap(lambda one_key: jax.random.permutation(one_key, TILES)[:K])(keys)
    return chosen.astype(jnp.int32)


def draw_replicas(key, part):
    partition_count = EDGE_PARTITIONS
    hot_dest = jax.random.randint(jax.random.fold_in(key, 1), (), 0, partition_count)
    offset = jax.random.randint(jax.random.fold_in(key, 2), (partition_count, 1), 0, partition_count)
    row_shift = jax.random.randint(jax.random.fold_in(key, 3), (partition_count, partition_count), 0, MAST)
    source = jnp.arange(partition_count)[:, None]
    mirror_row_index = jnp.arange(MIRROR_VERTICES)[None, :]
    lower_end = jnp.minimum(source, hot_dest)
    upper_end = jnp.maximum(source, hot_dest)
    remaining = mirror_row_index - CAP
    chosen = (remaining + offset) % (partition_count - 2)
    chosen = chosen + (chosen >= lower_end)
    chosen = chosen + (chosen >= upper_end)
    dest_cold = jnp.where(mirror_row_index < CAP, hot_dest, chosen)
    slot_cold = jnp.where(mirror_row_index < CAP, mirror_row_index, remaining // (partition_count - 2))
    chosen_hot = (mirror_row_index + offset) % (partition_count - 1)
    chosen_hot = chosen_hot + (chosen_hot >= source)
    slot_hot = mirror_row_index // (partition_count - 1)
    is_hot = source == hot_dest
    destination = jnp.where(is_hot, chosen_hot, dest_cold)
    slot_rank = jnp.where(is_hot, slot_hot, slot_cold)
    shift_here = row_shift[jnp.broadcast_to(source, destination.shape), destination]
    master_row = (slot_rank * 37 + shift_here) % MAST
    stacked_rows = jnp.stack([destination, slot_rank, master_row])
    return stacked_rows.reshape(3, partition_count * MIRROR_VERTICES).astype(jnp.int32)


def plant(drawn, rng, smallest, top_value):
    extent = drawn.shape
    spot = [jax.random.randint(jax.random.fold_in(rng, axis), (), 0, extent[axis]) for axis in range(len(extent))]
    drawn = drawn.at[tuple(spot)].set(smallest)
    longest = extent.index(max(extent))
    spot[longest] = (spot[longest] + 1) % extent[longest]
    return drawn.at[tuple(spot)].set(top_value)


def steps_of(own_key, extent, shards, smallest, top_value):
    def one(axis_at, shards_of):
        draws = jax.random.uniform(jax.random.fold_in(jax.random.fold_in(own_key, 6), axis_at), (shards_of,), jnp.float32, smallest / len(shards), top_value / len(shards))
        return jnp.repeat(jnp.exp(draws), extent[axis_at] // shards_of).reshape((-1,) + (1,) * (len(extent) - axis_at - 1))

    gain = one(*shards[0])
    for cut in shards[1:]:
        gain = gain * one(*cut)
    return gain


def centred(key, shape, width, most, cuts=(), held_as=jnp.bfloat16):
    gain = steps_of(key, shape, cuts, -0.22, 0.18) if cuts else 1.0
    entries = jax.random.normal(key, shape, jnp.float32) * width * gain
    return jnp.minimum(jnp.maximum(entries, -most), most).astype(held_as)


def setup_inputs(seed: int = 0) -> dict:
    key_of = jax.random.split(jax.random.key(seed), 10)
    features = centred(key_of[0], (FIN, NM), 1.0, 6.0, ((0, 4), (1, 64)))
    tile_mask = plant((jax.random.randint(key_of[1], (EDGE_PARTITIONS * TILES, K, TILE, TILE), 0, K * TILE // 24) < 1).astype(jnp.int32), jax.random.fold_in(key_of[1], 1), 0, 1)
    tile_cols = draw_tile_cols(jax.random.fold_in(key_of[9], 71), 0)
    replicas = draw_replicas(jax.random.fold_in(key_of[9], 71), 0)
    degree = plant(jax.random.randint(key_of[4], (NM,), K * TILE // 64, K * TILE // 16), jax.random.fold_in(key_of[4], 1), K * TILE // 64, (K * TILE // 16) - 1).astype(jnp.int32)
    self_one = centred(key_of[5], (FIN, HID), FIN ** -0.5, 0.5)
    neigh_one = centred(key_of[6], (FIN, HID), (FIN // 16) ** -0.5, 2.0)
    self_two = centred(key_of[7], (HID, HID), HID ** -0.5, 0.375)
    neigh_two = centred(key_of[8], (HID, HID), (HID // 16) ** -0.5, 1.5)
    return dict(features=features, tile_mask=tile_mask, tile_cols=tile_cols, replicas=replicas, degree=degree, self_one=self_one, neigh_one=neigh_one, self_two=self_two, neigh_two=neigh_two)


def aggregate_part(operands):
    local_values, masks, columns = operands
    feature_row_block = local_values.shape[0]
    tiled = local_values.astype(jnp.float32).reshape(feature_row_block, TILES, TILE)
    selected = jnp.take(tiled, columns, axis=1)
    summed = jnp.einsum("fiku,ikvu->fiv", selected, masks.astype(jnp.float32))
    return summed.reshape(feature_row_block, ROWS)


def layer(value_rows, tile_mask, tile_cols, replicas, degree, w_self, w_neigh):
    feature_row_block = value_rows.shape[0]
    flattened_index = (replicas[0] * MAST + replicas[2]).astype(jnp.int32)
    mirror_values = jnp.take(value_rows, flattened_index, axis=1).reshape(feature_row_block, EDGE_PARTITIONS, MIRROR_VERTICES)
    local_values = jnp.concatenate([value_rows.reshape(feature_row_block, EDGE_PARTITIONS, MAST), mirror_values], axis=2)
    partial_sum = lax.map(aggregate_part, (jnp.moveaxis(local_values, 1, 0), tile_mask.reshape(EDGE_PARTITIONS, TILES, K, TILE, TILE), tile_cols.reshape(EDGE_PARTITIONS, TILES, K)))
    own_part = jnp.moveaxis(partial_sum[:, :, :MAST], 0, 1).reshape(feature_row_block, EDGE_PARTITIONS * MAST)
    rounded_down = lax.optimization_barrier(partial_sum[:, :, MAST:].astype(jnp.bfloat16)).astype(jnp.float32)
    mirror_partition = jnp.moveaxis(rounded_down, 0, 1).reshape(feature_row_block, EDGE_PARTITIONS * MIRROR_VERTICES)
    total = own_part.at[:, flattened_index].add(mirror_partition)
    neighbours = (total / degree.astype(jnp.float32)[None, :]).astype(jnp.bfloat16)
    return jnp.dot(w_self.T, value_rows, preferred_element_type=jnp.float32) + jnp.dot(w_neigh.T, neighbours, preferred_element_type=jnp.float32)


def reference(features, tile_mask, tile_cols, replicas, degree, self_one, neigh_one, self_two, neigh_two):
    first = layer(features, tile_mask, tile_cols, replicas, degree, self_one, neigh_one)
    hidden = jax.nn.relu(first).astype(jnp.bfloat16)
    second = layer(hidden, tile_mask, tile_cols, replicas, degree, self_two, neigh_two)
    return second.astype(jnp.bfloat16)
```

```python
import jax
import jax.numpy as jnp
from jax import lax
from jax.experimental import pallas as pl
from jax.experimental.pallas import tpu as pltpu
from jax.sharding import PartitionSpec as P

F32, BF16, I32 = jnp.float32, jnp.bfloat16, jnp.int32
MESH = pl.DeviceIdType.MESH
LANES = 128
LO = 256
NN = (((1,), (0,)), ((), ()))
NT = (((1,), (1,)), ((), ()))


def dot(a, b, dims=NN):
    return lax.dot_general(a, b, dims, preferred_element_type=F32)


def kernel(
    doms, feats, cap,
    feat_ref, mask_ref, cols_ref, reps_ref, deg_ref, s1_ref, n1_ref, s2_ref, n2_ref,
    out_ref,
    stage, adj, gate_a, pick_a, gate_b, pick_b, want_out, want_in, whi,
    w1, w2, stacked, unfolded, local, own, mirror_part,
    total, hid, agg1, agg2, feat_all, hid_all, agg1_all, agg2_all,
    box_f1, box_r1, box_f2, box_r2, got_f1, got_r1, got_f2, got_r2,
    mask_sem, send_sem, recv_sem, feat_send, feat_recv,
):
    me, part = lax.axis_index("dom"), lax.axis_index("feat")
    blocks, per_row = cols_ref.shape
    tile = mask_ref.shape[-1]
    masters, mirrors = feat_ref.shape[1], reps_ref.shape[1]
    groups = doms * cap // LO
    each = LO // cap
    quarters = masters // LO
    master_blocks = masters // tile
    low = lax.broadcasted_iota(I32, (1, LANES), 1) < cap

    for i in range(blocks):
        pltpu.make_async_copy(mask_ref.at[i], stage.at[i], mask_sem.at[i]).start()

    barrier = pltpu.get_barrier_semaphore()

    def greet(d, _):
        pl.semaphore_signal(
            barrier, 1, device_id={"dom": lax.rem(me + d, doms)}, device_id_type=MESH
        )
        return 0

    lax.fori_loop(1, doms, greet, 0)
    for d in range(1, feats):
        pl.semaphore_signal(
            barrier, 1, device_id={"feat": lax.rem(part + d, feats)}, device_id_type=MESH
        )

    position = reps_ref[0:1, :] * cap + reps_ref[1:2, :]
    slot_group, slot_column = position >> 8, position & (LO - 1)
    for j in range(0, mirrors, LO):
        rows = lax.broadcasted_iota(I32, (LO, LO), 0)
        hit = rows == slot_column[:, j : j + LO]
        pick_b[:, j : j + LO] = jnp.where(hit, 1.0, 0.0).astype(BF16)
    for h in range(groups):
        hit = jnp.where(slot_group == h, 1.0, 0.0)
        gate_b[h] = jnp.broadcast_to(hit, (16, mirrors)).astype(BF16)

    row = reps_ref[2:3, :]
    kind = lax.broadcasted_iota(I32, (16, 1), 0)
    words = jnp.where(kind == 0, row & (LO - 1), jnp.where(kind == 1, (row >> 8) + 1, 0))
    words = words.astype(F32).astype(BF16)

    def name_rows(h, _):
        slots = dot(words * gate_b[h], pick_b[...], NT)
        value = slots[1:2] * float(LO) + slots[0:1]
        for c in range(LO // LANES):
            pair = value[:, c * LANES : (c + 1) * LANES]
            swapped = pltpu.roll(pair, cap, 1)
            want_out[each * h + 2 * c] = jnp.where(low, pair, 0.0)
            want_out[each * h + 2 * c + 1] = jnp.where(low, swapped, 0.0)
        return 0

    lax.fori_loop(0, groups, name_rows, 0)
    want_in[me] = jnp.zeros((1, LANES), F32)

    pl.semaphore_wait(barrier, doms - 1 + feats - 1)

    def send(box, got, which, q):
        @pl.when(q != me)
        def _():
            pltpu.make_async_remote_copy(
                src_ref=box.at[q],
                dst_ref=got.at[me],
                send_sem=send_sem.at[which],
                recv_sem=recv_sem.at[which],
                device_id={"dom": q},
                device_id_type=MESH,
            ).start()

    def arrived(got, which):
        rest = got.at[pl.ds(0, doms - 1)]
        pltpu.make_async_copy(rest, rest, recv_sem.at[which]).wait()

    def sent(box, which):
        rest = box.at[pl.ds(0, doms - 1)]
        pltpu.make_async_copy(rest, rest, send_sem.at[which]).wait()

    def share(mine, everyone, which):
        everyone[part] = mine[...]
        for d in range(1, feats):
            pltpu.make_async_remote_copy(
                src_ref=mine,
                dst_ref=everyone.at[part],
                send_sem=feat_send.at[which],
                recv_sem=feat_recv.at[which],
                device_id={"feat": lax.rem(part + d, feats)},
                device_id_type=MESH,
            ).start()

    def shared(everyone, which):
        rest = everyone.at[pl.ds(0, feats - 1)]
        pltpu.make_async_copy(rest, rest, feat_recv.at[which]).wait()

    def all_sent(everyone, which):
        rest = everyone.at[pl.ds(0, feats - 1)]
        pltpu.make_async_copy(rest, rest, feat_send.at[which]).wait()

    def ask(d, _):
        send(want_out, want_in, 0, lax.rem(me + d, doms))
        return 0

    lax.fori_loop(1, doms, ask, 0)
    share(feat_ref, feat_all, 0)

    width = w1.shape[0]
    column = lax.broadcasted_iota(I32, (width, s1_ref.shape[1]), 1)
    wanted = lax.broadcasted_iota(I32, column.shape, 0) + part * width
    choose = jnp.where(column == wanted, 1.0, 0.0).astype(BF16)
    fin, hdim = s1_ref.shape[0], s2_ref.shape[0]
    w1[:, :fin] = dot(choose, s1_ref[...], NT).astype(BF16)
    w1[:, fin:] = dot(choose, n1_ref[...], NT).astype(BF16)
    w2[:, :hdim] = dot(choose, s2_ref[...], NT).astype(BF16)
    w2[:, hdim:] = dot(choose, n2_ref[...], NT).astype(BF16)


    arrived(want_in, 0)

    def read_wants(g, _):
        parts = []
        for c in range(LO // LANES):
            even = want_in[each * g + 2 * c]
            odd = pltpu.roll(want_in[each * g + 2 * c + 1], cap, 1)
            parts.append(jnp.where(low, even, odd))
        value = jnp.concatenate(parts, axis=1).astype(I32)
        hit = lax.broadcasted_iota(I32, (LO, LO), 0) == (value & (LO - 1))
        pick_a[g] = jnp.where(hit, 1.0, 0.0).astype(BF16)
        quarter = value >> 8
        whi[g] = quarter
        for h in range(quarters):
            mine = jnp.where(quarter == h + 1, 1.0, 0.0)
            gate_a[g, h] = jnp.broadcast_to(mine, (16, LO)).astype(BF16)
        return 0

    lax.fori_loop(0, groups, read_wants, 0)

    def fold_and_send(values, box, got, which, g, n):
        half = n // 2
        for c in range(LO // LANES):
            pair = values[:, c * LANES : (c + 1) * LANES]
            top, bottom = pair[:half], pltpu.roll(pair[half:], cap, 1)
            even = jnp.where(low, top, bottom)
            odd = pltpu.roll(jnp.where(low, bottom, top), cap, 1)
            box[each * g + 2 * c] = even.astype(BF16)
            box[each * g + 2 * c + 1] = odd.astype(BF16)
        for i in range(each):
            send(box, got, which, each * g + lax.rem(me + i, each))

    def unfold(got, g):
        tops, bottoms = [], []
        for c in range(LO // LANES):
            even = got[each * g + 2 * c].astype(F32)
            odd = pltpu.roll(got[each * g + 2 * c + 1].astype(F32), cap, 1)
            tops.append(jnp.where(low, even, odd))
            bottoms.append(pltpu.roll(jnp.where(low, odd, even), cap, 1))
        top, bottom = jnp.concatenate(tops, axis=1), jnp.concatenate(bottoms, axis=1)
        return jnp.concatenate([top, bottom], axis=0).astype(BF16)

    def serve(values, n, box, got, which):
        got[me] = jnp.zeros(got.shape[1:], BF16)
        for h in range(quarters):
            stacked[pl.ds(h * n, n), :] = values[:, h * LO : (h + 1) * LO]

        def one(d, _):
            g = lax.rem(me // each + d, groups)
            found = dot(stacked[pl.ds(0, quarters * n), :], pick_a[g])
            quarter = whi[g]
            answer = jnp.zeros((n, LO), F32)
            for h in range(quarters):
                answer = jnp.where(quarter == h + 1, found[h * n : (h + 1) * n], answer)
            fold_and_send(answer, box, got, which, g, n)
            return 0

        lax.fori_loop(0, groups, one, 0)

    def place(values, got, which, n):
        for b in range(master_blocks):
            local[b, pl.ds(0, n), :] = values[:, b * tile : (b + 1) * tile]
        arrived(got, which)

        def open_up(g, _):
            unfolded[pl.ds(pl.multiple_of(g * n, n), n), :] = unfold(got, g)
            return 0

        lax.fori_loop(0, groups, open_up, 0)
        for j in range(mirrors // LO):
            column = pick_b[:, j * LO : (j + 1) * LO]
            group = slot_group[:, j * LO : (j + 1) * LO]
            found = dot(unfolded[pl.ds(0, groups * n), :], column)
            answer = jnp.zeros((n, LO), F32)
            for h in range(groups):
                answer = jnp.where(group == h, found[h * n : (h + 1) * n], answer)
            answer = answer.astype(BF16)
            for c in range(LO // tile):
                b = master_blocks + j * (LO // tile) + c
                local[b, pl.ds(0, n), :] = answer[:, c * tile : (c + 1) * tile]

    def aggregate(n):
        def row_block(i):
            sources = [local[cols_ref[i, k], pl.ds(0, n), :] for k in range(per_row)]
            return dot(jnp.concatenate(sources, axis=1), adj[i], NT)

        def of_masters(i, _):
            own[i, pl.ds(0, n), :] = row_block(i)
            return 0

        def of_mirrors(i, _):
            mirror_part[i - master_blocks, pl.ds(0, n), :] = row_block(i).astype(BF16)
            return 0

        lax.fori_loop(master_blocks, blocks, of_mirrors, 0)
        lax.fori_loop(0, master_blocks, of_masters, 0)

    def give_back(n, box, got, which):
        got[me] = jnp.zeros(got.shape[1:], BF16)
        step = 4
        sums = jnp.concatenate(
            [mirror_part[b, pl.ds(0, n), :] for b in range(mirrors // tile)], axis=1
        )

        def some(d, _):
            first = lax.rem(me // each // step + d, groups // step) * step
            rows = []
            for h in range(step):
                gate = gate_b[first + h]
                rows.append(sums * jnp.concatenate([gate] * (n // 16), axis=0))
            slots = dot(jnp.concatenate(rows, axis=0), pick_b[...], NT)
            for h in range(step):
                fold_and_send(slots[h * n : (h + 1) * n], box, got, which, first + h, n)
            return 0

        lax.fori_loop(0, groups // step, some, 0)

    def combine(n, got, which, mean):
        arrived(got, which)
        size = quarters * n
        total[pl.ds(0, size), :] = jnp.zeros((size, LO), F32)

        def one(g, _):
            values = unfold(got, g)
            rows = []
            for h in range(quarters):
                gate = gate_a[g, h]
                rows.append(values * jnp.concatenate([gate] * (n // 16), axis=0))
            total[pl.ds(0, size), :] += dot(jnp.concatenate(rows, axis=0), pick_a[g], NT)
            return 0

        lax.fori_loop(0, groups, one, 0)
        for b in range(master_blocks):
            h, c = divmod(b * tile, LO)
            sums = own[b, pl.ds(0, n), :] + total[pl.ds(h * n, n), c : c + tile]
            scale = deg_ref[:, b * tile : (b + 1) * tile].astype(F32)
            mean[:, b * tile : (b + 1) * tile] = (sums / scale).astype(BF16)

    def mix(weights, inputs, means):
        count = inputs.shape[0] * inputs.shape[1]
        result = dot(weights[:, :count], inputs[...].reshape(count, masters))
        return result + dot(weights[:, count:], means[...].reshape(count, masters))

    n1, n2 = feat_ref.shape[0], hid.shape[0]
    serve(feat_ref, n1, box_f1, got_f1, 1)

    def take_block(i, _):
        pltpu.make_async_copy(mask_ref.at[i], stage.at[i], mask_sem.at[i]).wait()
        for k in range(per_row):
            adj[i, :, k * tile : (k + 1) * tile] = stage[i, k].astype(F32).astype(BF16)
        return 0

    lax.fori_loop(0, blocks, take_block, 0)
    place(feat_ref, got_f1, 1, n1)
    aggregate(n1)
    give_back(n1, box_r1, got_r1, 2)
    combine(n1, got_r1, 2, agg1)
    share(agg1, agg1_all, 1)
    shared(feat_all, 0)
    shared(agg1_all, 1)
    hid[...] = jnp.maximum(mix(w1, feat_all, agg1_all), 0.0).astype(BF16)

    share(hid, hid_all, 2)
    serve(hid, n2, box_f2, got_f2, 3)
    place(hid, got_f2, 3, n2)
    aggregate(n2)
    give_back(n2, box_r2, got_r2, 4)
    combine(n2, got_r2, 4, agg2)
    share(agg2, agg2_all, 3)
    shared(hid_all, 2)
    shared(agg2_all, 3)
    out_ref[...] = mix(w2, hid_all, agg2_all).astype(BF16)

    sent(want_out, 0)
    for which, box in enumerate((box_f1, box_r1, box_f2, box_r2)):
        sent(box, which + 1)
    for which, everyone in enumerate((feat_all, agg1_all, hid_all, agg2_all)):
        all_sent(everyone, which)


def solution(mesh):
    doms, feats = mesh.shape["dom"], mesh.shape["feat"]

    def on_device(features, tile_mask, tile_cols, replicas, degree, s1, n1, s2, n2):
        rows, masters = features.shape
        mirrors = replicas.shape[1]
        cap = 2 * mirrors // doms
        blocks, per_row, tile, _ = tile_mask.shape
        wide = s1.shape[1] // feats
        groups, quarters = doms * cap // LO, masters // LO
        vmem = pl.BlockSpec(memory_space=pltpu.VMEM)
        box1 = pltpu.VMEM((doms, rows // 2, LANES), BF16)
        box2 = pltpu.VMEM((doms, wide // 2, LANES), BF16)
        dma = pltpu.SemaphoreType.DMA
        scratch = [
            pltpu.VMEM((blocks, per_row, tile, tile), I32),
            pltpu.VMEM((blocks, tile, per_row * tile), BF16),
            pltpu.VMEM((groups, quarters, 16, LO), BF16),
            pltpu.VMEM((groups, LO, LO), BF16),
            pltpu.VMEM((groups, 16, mirrors), BF16),
            pltpu.VMEM((LO, mirrors), BF16),
            pltpu.VMEM((doms, 1, LANES), F32),
            pltpu.VMEM((doms, 1, LANES), F32),
            pltpu.VMEM((groups, 1, LO), I32),
            pltpu.VMEM((wide, 2 * s1.shape[0]), BF16),
            pltpu.VMEM((wide, 2 * s2.shape[0]), BF16),
            pltpu.VMEM((quarters * wide, LO), BF16),
            pltpu.VMEM((groups * wide, LO), BF16),
            pltpu.VMEM((blocks, wide, tile), BF16),
            pltpu.VMEM((masters // tile, wide, tile), F32),
            pltpu.VMEM((mirrors // tile, wide, tile), BF16),
            pltpu.VMEM((quarters * wide, LO), F32),
            pltpu.VMEM((wide, masters), BF16),
            pltpu.VMEM((rows, masters), BF16),
            pltpu.VMEM((wide, masters), BF16),
            pltpu.VMEM((feats, rows, masters), BF16),
            pltpu.VMEM((feats, wide, masters), BF16),
            pltpu.VMEM((feats, rows, masters), BF16),
            pltpu.VMEM((feats, wide, masters), BF16),
            box1, box1, box2, box2, box1, box1, box2, box2,
            dma((blocks,)), dma((5,)), dma((5,)), dma((4,)), dma((4,)),
        ]
        return pl.pallas_call(
            lambda *refs: kernel(doms, feats, cap, *refs),
            name="two_layers",
            out_shape=jax.ShapeDtypeStruct((wide, masters), BF16),
            in_specs=[
                vmem,
                pl.BlockSpec(memory_space=pl.ANY),
                pl.BlockSpec(memory_space=pltpu.SMEM),
                vmem, vmem, vmem, vmem, vmem, vmem,
            ],
            out_specs=vmem,
            scratch_shapes=scratch,
            compiler_params=pltpu.CompilerParams(
                collective_id=0, has_side_effects=True, vmem_limit_bytes=56 << 20
            ),
        )(features, tile_mask, tile_cols, replicas, degree.reshape(1, masters), s1, n1, s2, n2)

    return jax.shard_map(
        on_device,
        mesh=mesh,
        in_specs=(
            P("feat", "dom"),
            P("dom", None, None, None),
            P("dom", None),
            P(None, "dom"),
            P("dom"),
            P(),
            P(),
            P(),
            P(),
        ),
        out_specs=P("feat", "dom"),
        check_vma=False,
    )
```

```python
import jax
import jax.numpy as jnp
from jax import lax
from jax.experimental import pallas as pl
from jax.experimental.pallas import tpu as pltpu
from jax.sharding import PartitionSpec as P

F32, BF16, I32 = jnp.float32, jnp.bfloat16, jnp.int32
MESH = pl.DeviceIdType.MESH
LANES = 128
UNROLL_TAKE, UNROLL_READ, UNROLL_SERVE, UNROLL_OPEN, UNROLL_AGG, UNROLL_COMB = 4, 4, 8, 8, 8, 8
LO = 256
NN = (((1,), (0,)), ((), ()))
NT = (((1,), (1,)), ((), ()))


def loop(first, last, unroll, body):
    def some(i, _):
        for u in range(unroll):
            body(first + i * unroll + u)
        return 0

    lax.fori_loop(0, (last - first) // unroll, some, 0)


def dot(a, b, dims=NN):
    return lax.dot_general(a, b, dims, preferred_element_type=F32)


def kernel(
    doms, feats, cap,
    feat_ref, mask_ref, cols_ref, reps_ref, deg_ref, s1_ref, n1_ref, s2_ref, n2_ref,
    out_ref,
    stage, adj, gate_a, pick_a, gate_b, pick_b, want_out, want_in, whi,
    w1, w2, stacked, unfolded, local, own, mirror_part,
    total, hid, agg1, agg2, feat_all, hid_all, agg1_all, agg2_all,
    box_f1, box_r1, box_f2, box_r2, got_f1, got_r1, got_f2, got_r2,
    mask_sem, send_sem, recv_sem, feat_send, feat_recv,
):
    me, part = lax.axis_index("dom"), lax.axis_index("feat")
    blocks, per_row = cols_ref.shape
    tile = mask_ref.shape[-1]
    masters, mirrors = feat_ref.shape[1], reps_ref.shape[1]
    groups = doms * cap // LO
    each = LO // cap
    quarters = masters // LO
    master_blocks = masters // tile
    low = lax.broadcasted_iota(I32, (1, LANES), 1) < cap

    for i in range(blocks):
        pltpu.make_async_copy(mask_ref.at[i], stage.at[i], mask_sem.at[i]).start()

    barrier = pltpu.get_barrier_semaphore()

    def greet(d, _):
        pl.semaphore_signal(
            barrier, 1, device_id={"dom": lax.rem(me + d, doms)}, device_id_type=MESH
        )
        return 0

    lax.fori_loop(1, doms, greet, 0)
    for d in range(1, feats):
        pl.semaphore_signal(
            barrier, 1, device_id={"feat": lax.rem(part + d, feats)}, device_id_type=MESH
        )

    position = reps_ref[0:1, :] * cap + reps_ref[1:2, :]
    slot_group, slot_column = position >> 8, position & (LO - 1)
    for j in range(0, mirrors, LO):
        rows = lax.broadcasted_iota(I32, (LO, LO), 0)
        hit = rows == slot_column[:, j : j + LO]
        pick_b[:, j : j + LO] = jnp.where(hit, 1.0, 0.0).astype(BF16)
    row = reps_ref[2:3, :]
    here = lax.broadcasted_iota(I32, (groups, mirrors), 0) == slot_group
    tails = jnp.where(here, row & (LO - 1), 0)
    heads = jnp.where(here, (row >> 8) + 1, 0)
    words = jnp.concatenate([tails, heads], axis=0).astype(F32).astype(BF16)
    slots = dot(words, pick_b[...], NT)
    slots = slots[groups:] * float(LO) + slots[:groups]
    for c in range(LO // LANES):
        pair = slots[:, c * LANES : (c + 1) * LANES]
        even = jnp.where(low, pair, 0.0)
        odd = jnp.where(low, pltpu.roll(pair, cap, 1), 0.0)
        for h in range(groups):
            want_out[each * h + 2 * c] = even[h : h + 1]
            want_out[each * h + 2 * c + 1] = odd[h : h + 1]
    want_in[me] = jnp.zeros((1, LANES), F32)

    pl.semaphore_wait(barrier, doms - 1 + feats - 1)

    def send(box, got, which, q):
        @pl.when(q != me)
        def _():
            pltpu.make_async_remote_copy(
                src_ref=box.at[q],
                dst_ref=got.at[me],
                send_sem=send_sem.at[which],
                recv_sem=recv_sem.at[which],
                device_id={"dom": q},
                device_id_type=MESH,
            ).start()

    def arrived(got, which):
        rest = got.at[pl.ds(0, doms - 1)]
        pltpu.make_async_copy(rest, rest, recv_sem.at[which]).wait()

    def sent(box, which):
        rest = box.at[pl.ds(0, doms - 1)]
        pltpu.make_async_copy(rest, rest, send_sem.at[which]).wait()

    def share(mine, everyone, which):
        everyone[part] = mine[...]
        for d in range(1, feats):
            pltpu.make_async_remote_copy(
                src_ref=mine,
                dst_ref=everyone.at[part],
                send_sem=feat_send.at[which],
                recv_sem=feat_recv.at[which],
                device_id={"feat": lax.rem(part + d, feats)},
                device_id_type=MESH,
            ).start()

    def shared(everyone, which):
        rest = everyone.at[pl.ds(0, feats - 1)]
        pltpu.make_async_copy(rest, rest, feat_recv.at[which]).wait()

    def all_sent(everyone, which):
        rest = everyone.at[pl.ds(0, feats - 1)]
        pltpu.make_async_copy(rest, rest, feat_send.at[which]).wait()

    def ask(d, _):
        send(want_out, want_in, 0, lax.rem(me + d, doms))
        return 0

    lax.fori_loop(1, doms, ask, 0)
    share(feat_ref, feat_all, 0)

    width = w1.shape[0]
    column = lax.broadcasted_iota(I32, (width, s1_ref.shape[1]), 1)
    wanted = lax.broadcasted_iota(I32, column.shape, 0) + part * width
    choose = jnp.where(column == wanted, 1.0, 0.0).astype(BF16)
    fin, hdim = s1_ref.shape[0], s2_ref.shape[0]
    w1[:, :fin] = dot(choose, s1_ref[...], NT).astype(BF16)
    w1[:, fin:] = dot(choose, n1_ref[...], NT).astype(BF16)
    w2[:, :hdim] = dot(choose, s2_ref[...], NT).astype(BF16)
    w2[:, hdim:] = dot(choose, n2_ref[...], NT).astype(BF16)


    for h in range(groups):
        hit = jnp.where(slot_group == h, 1.0, 0.0)
        gate_b[h] = jnp.broadcast_to(hit, (16, mirrors)).astype(BF16)

    def take_block(i):
        pltpu.make_async_copy(mask_ref.at[i], stage.at[i], mask_sem.at[i]).wait()
        for k in range(per_row):
            adj[i, :, k * tile : (k + 1) * tile] = stage[i, k].astype(F32).astype(BF16)

    loop(0, blocks, UNROLL_TAKE, take_block)
    arrived(want_in, 0)

    def read_wants(g):
        parts = []
        for c in range(LO // LANES):
            even = want_in[each * g + 2 * c]
            odd = pltpu.roll(want_in[each * g + 2 * c + 1], cap, 1)
            parts.append(jnp.where(low, even, odd))
        value = jnp.concatenate(parts, axis=1).astype(I32)
        hit = lax.broadcasted_iota(I32, (LO, LO), 0) == (value & (LO - 1))
        pick_a[g] = jnp.where(hit, 1.0, 0.0).astype(BF16)
        quarter = value >> 8
        whi[g] = quarter
        for h in range(quarters):
            mine = jnp.where(quarter == h + 1, 1.0, 0.0)
            gate_a[g, h] = jnp.broadcast_to(mine, (16, LO)).astype(BF16)

    loop(0, groups, UNROLL_READ, read_wants)

    def fold(values, box, g, n):
        half = n // 2
        for c in range(LO // LANES):
            pair = values[:, c * LANES : (c + 1) * LANES]
            top, bottom = pair[:half], pltpu.roll(pair[half:], cap, 1)
            even = jnp.where(low, top, bottom)
            odd = pltpu.roll(jnp.where(low, bottom, top), cap, 1)
            box[each * g + 2 * c] = even.astype(BF16)
            box[each * g + 2 * c + 1] = odd.astype(BF16)

    def send_group(box, got, which, g):
        for i in range(each):
            send(box, got, which, each * g + lax.rem(me + i, each))

    def unfold(got, g):
        tops, bottoms = [], []
        for c in range(LO // LANES):
            even = got[each * g + 2 * c].astype(F32)
            odd = pltpu.roll(got[each * g + 2 * c + 1].astype(F32), cap, 1)
            tops.append(jnp.where(low, even, odd))
            bottoms.append(pltpu.roll(jnp.where(low, odd, even), cap, 1))
        top, bottom = jnp.concatenate(tops, axis=1), jnp.concatenate(bottoms, axis=1)
        return jnp.concatenate([top, bottom], axis=0).astype(BF16)

    def serve(values, n, box, got, which):
        got[me] = jnp.zeros(got.shape[1:], BF16)
        for h in range(quarters):
            stacked[pl.ds(h * n, n), :] = values[:, h * LO : (h + 1) * LO]

        rows = stacked[pl.ds(0, quarters * n), :]

        def some(d, _):
            these = [lax.rem(me // each + d * UNROLL_SERVE + u, groups) for u in range(UNROLL_SERVE)]
            found = [dot(rows, pick_a[g]) for g in these]
            for g, f in zip(these, found):
                quarter = whi[g]
                answer = jnp.zeros((n, LO), F32)
                for h in range(quarters):
                    answer = jnp.where(quarter == h + 1, f[h * n : (h + 1) * n], answer)
                fold(answer, box, g, n)
            for g in these:
                send_group(box, got, which, g)
            return 0

        lax.fori_loop(0, groups // UNROLL_SERVE, some, 0)

    def place(values, got, which, n):
        for b in range(master_blocks):
            local[b, pl.ds(0, n), :] = values[:, b * tile : (b + 1) * tile]
        arrived(got, which)

        def open_up(g):
            unfolded[pl.ds(pl.multiple_of(g * n, n), n), :] = unfold(got, g)

        loop(0, groups, UNROLL_OPEN, open_up)
        for j in range(mirrors // LO):
            column = pick_b[:, j * LO : (j + 1) * LO]
            group = slot_group[:, j * LO : (j + 1) * LO]
            found = dot(unfolded[pl.ds(0, groups * n), :], column)
            answer = jnp.zeros((n, LO), F32)
            for h in range(groups):
                answer = jnp.where(group == h, found[h * n : (h + 1) * n], answer)
            answer = answer.astype(BF16)
            for c in range(LO // tile):
                b = master_blocks + j * (LO // tile) + c
                local[b, pl.ds(0, n), :] = answer[:, c * tile : (c + 1) * tile]

    def aggregate(n):
        def row_block(i):
            sources = [local[cols_ref[i, k], pl.ds(0, n), :] for k in range(per_row)]
            return dot(jnp.concatenate(sources, axis=1), adj[i], NT)

        def of_masters(d, _):
            these = [d * UNROLL_AGG + u for u in range(UNROLL_AGG)]
            for i, sums in [(i, row_block(i)) for i in these]:
                own[i, pl.ds(0, n), :] = sums
            return 0

        def of_mirrors(d, _):
            these = [d * UNROLL_AGG + u for u in range(UNROLL_AGG)]
            for i, sums in [(i, row_block(i + master_blocks)) for i in these]:
                mirror_part[i, pl.ds(0, n), :] = sums.astype(BF16)
            return 0

        lax.fori_loop(0, (blocks - master_blocks) // UNROLL_AGG, of_mirrors, 0)
        lax.fori_loop(0, master_blocks // UNROLL_AGG, of_masters, 0)

    def give_back(n, box, got, which):
        got[me] = jnp.zeros(got.shape[1:], BF16)
        step = 4
        sums = jnp.concatenate(
            [mirror_part[b, pl.ds(0, n), :] for b in range(mirrors // tile)], axis=1
        )

        def some(d, _):
            first = lax.rem(me // each // step + d, groups // step) * step
            rows = []
            for h in range(step):
                gate = gate_b[first + h]
                rows.append(sums * jnp.concatenate([gate] * (n // 16), axis=0))
            slots = dot(jnp.concatenate(rows, axis=0), pick_b[...], NT)
            for h in range(step):
                fold(slots[h * n : (h + 1) * n], box, first + h, n)
            for h in range(step):
                send_group(box, got, which, first + h)
            return 0

        lax.fori_loop(0, groups // step, some, 0)

    def combine(n, got, which, mean):
        arrived(got, which)
        size = quarters * n
        total[pl.ds(0, size), :] = jnp.zeros((size, LO), F32)

        def some(d, _):
            sums = []
            for g in [d * UNROLL_COMB + u for u in range(UNROLL_COMB)]:
                values = unfold(got, g)
                rows = []
                for h in range(quarters):
                    gate = gate_a[g, h]
                    rows.append(values * jnp.concatenate([gate] * (n // 16), axis=0))
                sums.append(dot(jnp.concatenate(rows, axis=0), pick_a[g], NT))
            total[pl.ds(0, size), :] += sum(sums[1:], sums[0])
            return 0

        lax.fori_loop(0, groups // UNROLL_COMB, some, 0)
        for b in range(master_blocks):
            h, c = divmod(b * tile, LO)
            sums = own[b, pl.ds(0, n), :] + total[pl.ds(h * n, n), c : c + tile]
            scale = deg_ref[:, b * tile : (b + 1) * tile].astype(F32)
            mean[:, b * tile : (b + 1) * tile] = (sums / scale).astype(BF16)

    def mix(weights, inputs, means):
        count = inputs.shape[0] * inputs.shape[1]
        result = dot(weights[:, :count], inputs[...].reshape(count, masters))
        return result + dot(weights[:, count:], means[...].reshape(count, masters))

    n1, n2 = feat_ref.shape[0], hid.shape[0]
    serve(feat_ref, n1, box_f1, got_f1, 1)

    place(feat_ref, got_f1, 1, n1)
    aggregate(n1)
    give_back(n1, box_r1, got_r1, 2)
    combine(n1, got_r1, 2, agg1)
    share(agg1, agg1_all, 1)
    shared(feat_all, 0)
    shared(agg1_all, 1)
    hid[...] = jnp.maximum(mix(w1, feat_all, agg1_all), 0.0).astype(BF16)

    share(hid, hid_all, 2)
    serve(hid, n2, box_f2, got_f2, 3)
    place(hid, got_f2, 3, n2)
    aggregate(n2)
    give_back(n2, box_r2, got_r2, 4)
    combine(n2, got_r2, 4, agg2)
    share(agg2, agg2_all, 3)
    shared(hid_all, 2)
    shared(agg2_all, 3)
    out_ref[...] = mix(w2, hid_all, agg2_all).astype(BF16)

    sent(want_out, 0)
    for which, box in enumerate((box_f1, box_r1, box_f2, box_r2)):
        sent(box, which + 1)
    for which, everyone in enumerate((feat_all, agg1_all, hid_all, agg2_all)):
        all_sent(everyone, which)


def solution(mesh):
    doms, feats = mesh.shape["dom"], mesh.shape["feat"]

    def on_device(features, tile_mask, tile_cols, replicas, degree, s1, n1, s2, n2):
        rows, masters = features.shape
        mirrors = replicas.shape[1]
        cap = 2 * mirrors // doms
        blocks, per_row, tile, _ = tile_mask.shape
        wide = s1.shape[1] // feats
        groups, quarters = doms * cap // LO, masters // LO
        vmem = pl.BlockSpec(memory_space=pltpu.VMEM)
        box1 = pltpu.VMEM((doms, rows // 2, LANES), BF16)
        box2 = pltpu.VMEM((doms, wide // 2, LANES), BF16)
        dma = pltpu.SemaphoreType.DMA
        scratch = [
            pltpu.VMEM((blocks, per_row, tile, tile), I32),
            pltpu.VMEM((blocks, tile, per_row * tile), BF16),
            pltpu.VMEM((groups, quarters, 16, LO), BF16),
            pltpu.VMEM((groups, LO, LO), BF16),
            pltpu.VMEM((groups, 16, mirrors), BF16),
            pltpu.VMEM((LO, mirrors), BF16),
            pltpu.VMEM((doms, 1, LANES), F32),
            pltpu.VMEM((doms, 1, LANES), F32),
            pltpu.VMEM((groups, 1, LO), I32),
            pltpu.VMEM((wide, 2 * s1.shape[0]), BF16),
            pltpu.VMEM((wide, 2 * s2.shape[0]), BF16),
            pltpu.VMEM((quarters * wide, LO), BF16),
            pltpu.VMEM((groups * wide, LO), BF16),
            pltpu.VMEM((blocks, wide, tile), BF16),
            pltpu.VMEM((masters // tile, wide, tile), F32),
            pltpu.VMEM((mirrors // tile, wide, tile), BF16),
            pltpu.VMEM((quarters * wide, LO), F32),
            pltpu.VMEM((wide, masters), BF16),
            pltpu.VMEM((rows, masters), BF16),
            pltpu.VMEM((wide, masters), BF16),
            pltpu.VMEM((feats, rows, masters), BF16),
            pltpu.VMEM((feats, wide, masters), BF16),
            pltpu.VMEM((feats, rows, masters), BF16),
            pltpu.VMEM((feats, wide, masters), BF16),
            box1, box1, box2, box2, box1, box1, box2, box2,
            dma((blocks,)), dma((5,)), dma((5,)), dma((4,)), dma((4,)),
        ]
        return pl.pallas_call(
            lambda *refs: kernel(doms, feats, cap, *refs),
            name="two_layers",
            out_shape=jax.ShapeDtypeStruct((wide, masters), BF16),
            in_specs=[
                vmem,
                pl.BlockSpec(memory_space=pl.ANY),
                pl.BlockSpec(memory_space=pltpu.SMEM),
                vmem, vmem, vmem, vmem, vmem, vmem,
            ],
            out_specs=vmem,
            scratch_shapes=scratch,
            compiler_params=pltpu.CompilerParams(
                collective_id=0, has_side_effects=True, vmem_limit_bytes=56 << 20
            ),
        )(features, tile_mask, tile_cols, replicas, degree.reshape(1, masters), s1, n1, s2, n2)

    return jax.shard_map(
        on_device,
        mesh=mesh,
        in_specs=(
            P("feat", "dom"),
            P("dom", None, None, None),
            P("dom", None),
            P(None, "dom"),
            P("dom"),
            P(),
            P(),
            P(),
            P(),
        ),
        out_specs=P("feat", "dom"),
        check_vma=False,
    )
```

```python
import jax
import jax.numpy as jnp
from jax import lax
from jax.experimental import pallas as pl
from jax.experimental.pallas import tpu as pltpu
from jax.sharding import PartitionSpec as P

F32, BF16, I32 = jnp.float32, jnp.bfloat16, jnp.int32
MESH = pl.DeviceIdType.MESH
LANES = 128
PARTS1, PARTS2 = 2, 2
UNROLL_TAKE, UNROLL_READ, UNROLL_SERVE, UNROLL_OPEN, UNROLL_AGG, UNROLL_COMB = 4, 4, 8, 8, 8, 8
LO = 256
NN = (((1,), (0,)), ((), ()))
NT = (((1,), (1,)), ((), ()))


def loop(first, last, unroll, body):
    def some(i, _):
        for u in range(unroll):
            body(first + i * unroll + u)
        return 0

    lax.fori_loop(0, (last - first) // unroll, some, 0)


def dot(a, b, dims=NN):
    return lax.dot_general(a, b, dims, preferred_element_type=F32)


def kernel(
    doms, feats, cap,
    feat_hbm, mask_ref, cols_ref, reps_ref, deg_hbm, s1_hbm, n1_hbm, s2_hbm, n2_hbm,
    out_ref,
    feat_ref, deg_ref, s1_ref, n1_ref, s2_ref, n2_ref,
    stage, adj, gate_a, pick_a, gate_b, pick_b, want_out, want_in, whi,
    w1s, w1n, w2s, w2n, stacked, unfolded, local, own1, own2, mirror_part,
    total, plain, hid, agg1, agg2, feat_all, hid_all, agg1_all, agg2_all,
    box_f1, box_r1, box_f2, box_r2, got_f1, got_r1, got_f2, got_r2,
    in_sem, mask_sem, send_sem, recv_sem, feat_send, feat_recv,
):
    me, part = lax.axis_index("dom"), lax.axis_index("feat")
    per_row, blocks = cols_ref.shape
    tile = mask_ref.shape[-1]
    masters, mirrors = feat_ref.shape[1], reps_ref.shape[1]
    groups = doms * cap // LO
    each = LO // cap
    quarters = masters // LO
    master_blocks = masters // tile
    low = lax.broadcasted_iota(I32, (1, LANES), 1) < cap

    barrier = pltpu.get_barrier_semaphore()

    def greet(d, _):
        pl.semaphore_signal(
            barrier, 1, device_id={"dom": lax.rem(me + d, doms)}, device_id_type=MESH
        )
        return 0

    lax.fori_loop(1, doms, greet, 0)
    for d in range(1, feats):
        pl.semaphore_signal(
            barrier, 1, device_id={"feat": lax.rem(part + d, feats)}, device_id_type=MESH
        )

    inputs = [
        pltpu.make_async_copy(source, target, in_sem.at[i])
        for i, (source, target) in enumerate(
            (
                (feat_hbm, feat_ref), (s1_hbm, s1_ref), (n1_hbm, n1_ref),
                (s2_hbm, s2_ref), (n2_hbm, n2_ref), (deg_hbm, deg_ref),
            )
        )
    ]
    for copy in inputs:
        copy.start()
    for i in range(blocks):
        pltpu.make_async_copy(mask_ref.at[i], stage.at[i], mask_sem.at[i]).start()

    position = reps_ref[0:1, :] * cap + reps_ref[1:2, :]
    slot_group, slot_column = position >> 8, position & (LO - 1)
    for j in range(0, mirrors, LO):
        rows = lax.broadcasted_iota(I32, (LO, LO), 0)
        hit = rows == slot_column[:, j : j + LO]
        pick_b[:, j : j + LO] = jnp.where(hit, 1.0, 0.0).astype(BF16)
    row = reps_ref[2:3, :]
    here = lax.broadcasted_iota(I32, (groups, mirrors), 0) == slot_group
    tails = jnp.where(here, row & (LO - 1), 0)
    heads = jnp.where(here, (row >> 8) + 1, 0)
    words = jnp.concatenate([tails, heads], axis=0).astype(F32).astype(BF16)
    slots = dot(words, pick_b[...], NT)
    slots = slots[groups:] * float(LO) + slots[:groups]
    for c in range(LO // LANES):
        pair = slots[:, c * LANES : (c + 1) * LANES]
        even = jnp.where(low, pair, 0.0)
        odd = jnp.where(low, pltpu.roll(pair, cap, 1), 0.0)
        for h in range(groups):
            want_out[each * h + 2 * c] = even[h : h + 1]
            want_out[each * h + 2 * c + 1] = odd[h : h + 1]
    want_in[me] = jnp.zeros((1, LANES), F32)

    pl.semaphore_wait(barrier, doms - 1 + feats - 1)

    def send(box, got, which, q):
        @pl.when(q != me)
        def _():
            pltpu.make_async_remote_copy(
                src_ref=box.at[q],
                dst_ref=got.at[me],
                send_sem=send_sem.at[which],
                recv_sem=recv_sem.at[which],
                device_id={"dom": q},
                device_id_type=MESH,
            ).start()

    def arrived(got, which):
        rest = got.at[pl.ds(0, doms - 1)]
        pltpu.make_async_copy(rest, rest, recv_sem.at[which]).wait()

    def sent(box, which):
        rest = box.at[pl.ds(0, doms - 1)]
        pltpu.make_async_copy(rest, rest, send_sem.at[which]).wait()

    def share(mine, everyone, which):
        everyone[part] = mine[...]
        for d in range(1, feats):
            pltpu.make_async_remote_copy(
                src_ref=mine,
                dst_ref=everyone.at[part],
                send_sem=feat_send.at[which],
                recv_sem=feat_recv.at[which],
                device_id={"feat": lax.rem(part + d, feats)},
                device_id_type=MESH,
            ).start()

    def shared(everyone, which):
        rest = everyone.at[pl.ds(0, feats - 1)]
        pltpu.make_async_copy(rest, rest, feat_recv.at[which]).wait()

    def all_sent(everyone, which):
        rest = everyone.at[pl.ds(0, feats - 1)]
        pltpu.make_async_copy(rest, rest, feat_send.at[which]).wait()

    def ask(d, _):
        send(want_out, want_in, 0, lax.rem(me + d, doms))
        return 0

    lax.fori_loop(1, doms, ask, 0)
    for copy in inputs:
        copy.wait()
    share(feat_ref, feat_all, 0)

    width = w1s.shape[0]
    column = lax.broadcasted_iota(I32, (width, s1_ref.shape[1]), 1)
    wanted = lax.broadcasted_iota(I32, column.shape, 0) + part * width
    choose = jnp.where(column == wanted, 1.0, 0.0).astype(BF16)
    w1s[...] = dot(choose, s1_ref[...], NT).astype(BF16)
    w2s[...] = dot(choose, s2_ref[...], NT).astype(BF16)
    for source, target in ((n1_ref, w1n), (n2_ref, w2n)):
        mine = source.shape[0] // feats
        for a in range(target.shape[0]):
            n = mine // target.shape[0]
            rows = [source[f * mine + a * n : f * mine + (a + 1) * n] for f in range(feats)]
            target[a] = dot(choose, jnp.concatenate(rows, axis=0), NT).astype(BF16)

    for h in range(groups):
        hit = jnp.where(slot_group == h, 1.0, 0.0)
        gate_b[h] = jnp.broadcast_to(hit, (16, mirrors)).astype(BF16)

    def take_block(i):
        pltpu.make_async_copy(mask_ref.at[i], stage.at[i], mask_sem.at[i]).wait()
        for k in range(per_row):
            adj[i, :, k * tile : (k + 1) * tile] = stage[i, k].astype(F32).astype(BF16)

    loop(0, blocks, UNROLL_TAKE, take_block)
    arrived(want_in, 0)

    def read_wants(g):
        parts = []
        for c in range(LO // LANES):
            even = want_in[each * g + 2 * c]
            odd = pltpu.roll(want_in[each * g + 2 * c + 1], cap, 1)
            parts.append(jnp.where(low, even, odd))
        value = jnp.concatenate(parts, axis=1).astype(I32)
        hit = lax.broadcasted_iota(I32, (LO, LO), 0) == (value & (LO - 1))
        pick_a[g] = jnp.where(hit, 1.0, 0.0).astype(BF16)
        quarter = value >> 8
        whi[g] = quarter
        for h in range(quarters):
            mine = jnp.where(quarter == h + 1, 1.0, 0.0)
            gate_a[g, h] = jnp.broadcast_to(mine, (16, LO)).astype(BF16)

    loop(0, groups, UNROLL_READ, read_wants)

    def fold(values, box, g, n):
        half = n // 2
        for c in range(LO // LANES):
            pair = values[:, c * LANES : (c + 1) * LANES]
            top, bottom = pair[:half], pltpu.roll(pair[half:], cap, 1)
            even = jnp.where(low, top, bottom)
            odd = pltpu.roll(jnp.where(low, bottom, top), cap, 1)
            box[each * g + 2 * c] = even.astype(BF16)
            box[each * g + 2 * c + 1] = odd.astype(BF16)

    def send_group(box, got, which, g):
        for i in range(each):
            send(box, got, which, each * g + lax.rem(me + i, each))

    def unfold(got, g):
        tops, bottoms = [], []
        for c in range(LO // LANES):
            even = got[each * g + 2 * c].astype(F32)
            odd = pltpu.roll(got[each * g + 2 * c + 1].astype(F32), cap, 1)
            tops.append(jnp.where(low, even, odd))
            bottoms.append(pltpu.roll(jnp.where(low, odd, even), cap, 1))
        top, bottom = jnp.concatenate(tops, axis=1), jnp.concatenate(bottoms, axis=1)
        return jnp.concatenate([top, bottom], axis=0).astype(BF16)

    def serve(values, n, box, got, which):
        got[me] = jnp.zeros((n // 2, LANES), BF16)
        for h in range(quarters):
            stacked[pl.ds(h * n, n), :] = values[:, h * LO : (h + 1) * LO]

        rows = stacked[pl.ds(0, quarters * n), :]

        def some(d, _):
            these = [lax.rem(me // each + d * UNROLL_SERVE + u, groups) for u in range(UNROLL_SERVE)]
            found = [dot(rows, pick_a[g]) for g in these]
            for g, f in zip(these, found):
                quarter = whi[g]
                answer = jnp.zeros((n, LO), F32)
                for h in range(quarters):
                    answer = jnp.where(quarter == h + 1, f[h * n : (h + 1) * n], answer)
                fold(answer, box, g, n)
            for g in these:
                send_group(box, got, which, g)
            return 0

        lax.fori_loop(0, groups // UNROLL_SERVE, some, 0)

    def place(values, got, which, n):
        for b in range(master_blocks):
            local[b, pl.ds(0, n), :] = values[:, b * tile : (b + 1) * tile]
        arrived(got, which)

        def open_up(g):
            unfolded[pl.ds(pl.multiple_of(g * n, n), n), :] = unfold(got, g)

        loop(0, groups, UNROLL_OPEN, open_up)
        for j in range(mirrors // LO):
            column = pick_b[:, j * LO : (j + 1) * LO]
            group = slot_group[:, j * LO : (j + 1) * LO]
            found = dot(unfolded[pl.ds(0, groups * n), :], column)
            answer = jnp.zeros((n, LO), F32)
            for h in range(groups):
                answer = jnp.where(group == h, found[h * n : (h + 1) * n], answer)
            answer = answer.astype(BF16)
            for c in range(LO // tile):
                b = master_blocks + j * (LO // tile) + c
                local[b, pl.ds(0, n), :] = answer[:, c * tile : (c + 1) * tile]

    def aggregate(n, own):
        def row_block(i):
            sources = [local[cols_ref[k, i], pl.ds(0, n), :] for k in range(per_row)]
            return dot(jnp.concatenate(sources, axis=1), adj[i], NT)

        def of_masters(d, _):
            these = [d * UNROLL_AGG + u for u in range(UNROLL_AGG)]
            for i, sums in [(i, row_block(i)) for i in these]:
                own[i] = sums
            return 0

        def of_mirrors(d, _):
            these = [d * UNROLL_AGG + u for u in range(UNROLL_AGG)]
            for i, sums in [(i, row_block(i + master_blocks)) for i in these]:
                mirror_part[i, pl.ds(0, n), :] = sums.astype(BF16)
            return 0

        lax.fori_loop(0, (blocks - master_blocks) // UNROLL_AGG, of_mirrors, 0)
        lax.fori_loop(0, master_blocks // UNROLL_AGG, of_masters, 0)

    def give_back(n, box, got, which):
        got[me] = jnp.zeros((n // 2, LANES), BF16)
        step = 4
        sums = jnp.concatenate(
            [mirror_part[b, pl.ds(0, n), :] for b in range(mirrors // tile)], axis=1
        )

        def some(d, _):
            first = lax.rem(me // each // step + d, groups // step) * step
            rows = []
            for h in range(step):
                gate = gate_b[first + h]
                rows.append(sums * jnp.concatenate([gate] * (n // 16), axis=0))
            slots = dot(jnp.concatenate(rows, axis=0), pick_b[...], NT)
            for h in range(step):
                fold(slots[h * n : (h + 1) * n], box, first + h, n)
            for h in range(step):
                send_group(box, got, which, first + h)
            return 0

        lax.fori_loop(0, groups // step, some, 0)

    def combine(n, own, got, which, mean):
        arrived(got, which)
        size = quarters * n
        total[pl.ds(0, size), :] = jnp.zeros((size, LO), F32)

        def some(d, _):
            sums = []
            for g in [d * UNROLL_COMB + u for u in range(UNROLL_COMB)]:
                values = unfold(got, g)
                rows = []
                for h in range(quarters):
                    gate = gate_a[g, h]
                    rows.append(values * jnp.concatenate([gate] * (n // 16), axis=0))
                sums.append(dot(jnp.concatenate(rows, axis=0), pick_a[g], NT))
            total[pl.ds(0, size), :] += sum(sums[1:], sums[0])
            return 0

        lax.fori_loop(0, groups // UNROLL_COMB, some, 0)
        for b in range(master_blocks):
            h, c = divmod(b * tile, LO)
            sums = own[b] + total[pl.ds(h * n, n), c : c + tile]
            scale = deg_ref[:, b * tile : (b + 1) * tile].astype(F32)
            mean[:, b * tile : (b + 1) * tile] = (sums / scale).astype(BF16)

    def mix_own(weights, inputs, which):
        shared(inputs, which)
        count = inputs.shape[0] * inputs.shape[1]
        plain[...] = dot(weights[...], inputs[...].reshape(count, masters))

    def mix_mean(weights, means, first, n):
        result = plain[first : first + n]
        for a in range(weights.shape[0]):
            count = means.shape[1] * means.shape[2]
            result += dot(weights[a, first : first + n, :], means[a].reshape(count, masters))
        return result

    def layer(values, weights, inputs, which_in, own, mean, means, which, f, r, first_share):
        count, n = mean.shape[:2]
        for a in range(count):
            place(values[a * n : (a + 1) * n], f[1].at[a], which + a, n)
            aggregate(n, own.at[a])
            give_back(n, r[0].at[a], r[1].at[a], which + count + a)
        mix_own(weights, inputs, which_in)
        for a in range(count):
            combine(n, own.at[a], r[1].at[a], which + count + a, mean.at[a])
            share(mean.at[a], means.at[a], first_share + a)
        for a in range(count):
            shared(means.at[a], first_share + a)

    parts1, n1 = agg1.shape[:2]
    parts2, n2 = agg2.shape[:2]
    base2, share2 = 1 + 2 * parts1, 2 + parts1
    boxes1, boxes2 = (box_f1, got_f1), (box_f2, got_f2)
    back1, back2 = (box_r1, got_r1), (box_r2, got_r2)
    for a in range(parts1):
        serve(feat_ref[a * n1 : (a + 1) * n1], n1, box_f1.at[a], got_f1.at[a], 1 + a)
    layer(feat_ref, w1s, feat_all, 0, own1, agg1, agg1_all, 1, boxes1, back1, 2)
    for a in range(parts2):
        rows = jnp.maximum(mix_mean(w1n, agg1_all, a * n2, n2), 0.0).astype(BF16)
        hid[a * n2 : (a + 1) * n2] = rows
        serve(hid[a * n2 : (a + 1) * n2], n2, box_f2.at[a], got_f2.at[a], base2 + a)
    share(hid, hid_all, 1)
    layer(hid, w2s, hid_all, 1, own2, agg2, agg2_all, base2, boxes2, back2, share2)
    out_ref[...] = mix_mean(w2n, agg2_all, 0, width).astype(BF16)

    sent(want_out, 0)
    which = 1
    for box in (box_f1, box_r1, box_f2, box_r2):
        for a in range(box.shape[0]):
            sent(box.at[a], which)
            which += 1
    all_sent(feat_all, 0)
    all_sent(hid_all, 1)
    which = 2
    for means in (agg1_all, agg2_all):
        for a in range(means.shape[0]):
            all_sent(means.at[a], which)
            which += 1


def solution(mesh):
    doms, feats = mesh.shape["dom"], mesh.shape["feat"]

    def on_device(features, tile_mask, tile_cols, replicas, degree, s1, n1, s2, n2):
        rows, masters = features.shape
        mirrors = replicas.shape[1]
        cap = 2 * mirrors // doms
        blocks, per_row, tile, _ = tile_mask.shape
        wide = s1.shape[1] // feats
        groups, quarters = doms * cap // LO, masters // LO
        c1, c2 = rows // PARTS1, wide // PARTS2
        most = max(c1, c2)
        vmem = pl.BlockSpec(memory_space=pltpu.VMEM)
        hbm = pl.BlockSpec(memory_space=pl.ANY)
        box1 = pltpu.VMEM((PARTS1, doms, c1 // 2, LANES), BF16)
        box2 = pltpu.VMEM((PARTS2, doms, c2 // 2, LANES), BF16)
        dma = pltpu.SemaphoreType.DMA
        exchanges, shares = 1 + 2 * (PARTS1 + PARTS2), 2 + PARTS1 + PARTS2
        scratch = [
            pltpu.VMEM(features.shape, BF16),
            pltpu.VMEM((1, masters), I32),
            *(pltpu.VMEM(w.shape, BF16) for w in (s1, n1, s2, n2)),
            pltpu.VMEM((blocks, per_row, tile, tile), I32),
            pltpu.VMEM((blocks, tile, per_row * tile), BF16),
            pltpu.VMEM((groups, quarters, 16, LO), BF16),
            pltpu.VMEM((groups, LO, LO), BF16),
            pltpu.VMEM((groups, 16, mirrors), BF16),
            pltpu.VMEM((LO, mirrors), BF16),
            pltpu.VMEM((doms, 1, LANES), F32),
            pltpu.VMEM((doms, 1, LANES), F32),
            pltpu.VMEM((groups, 1, LO), I32),
            pltpu.VMEM((wide, s1.shape[0]), BF16),
            pltpu.VMEM((PARTS1, wide, n1.shape[0] // PARTS1), BF16),
            pltpu.VMEM((wide, s2.shape[0]), BF16),
            pltpu.VMEM((PARTS2, wide, n2.shape[0] // PARTS2), BF16),
            pltpu.VMEM((quarters * most, LO), BF16),
            pltpu.VMEM((groups * most, LO), BF16),
            pltpu.VMEM((blocks, most, tile), BF16),
            pltpu.VMEM((PARTS1, masters // tile, c1, tile), F32),
            pltpu.VMEM((PARTS2, masters // tile, c2, tile), F32),
            pltpu.VMEM((mirrors // tile, most, tile), BF16),
            pltpu.VMEM((quarters * most, LO), F32),
            pltpu.VMEM((wide, masters), F32),
            pltpu.VMEM((wide, masters), BF16),
            pltpu.VMEM((PARTS1, c1, masters), BF16),
            pltpu.VMEM((PARTS2, c2, masters), BF16),
            pltpu.VMEM((feats, rows, masters), BF16),
            pltpu.VMEM((feats, wide, masters), BF16),
            pltpu.VMEM((PARTS1, feats, c1, masters), BF16),
            pltpu.VMEM((PARTS2, feats, c2, masters), BF16),
            box1, box1, box2, box2, box1, box1, box2, box2,
            dma((6,)), dma((blocks,)), dma((exchanges,)), dma((exchanges,)),
            dma((shares,)), dma((shares,)),
        ]
        return pl.pallas_call(
            lambda *refs: kernel(doms, feats, cap, *refs),
            name="two_layers",
            out_shape=jax.ShapeDtypeStruct((wide, masters), BF16),
            in_specs=[
                hbm, hbm, pl.BlockSpec(memory_space=pltpu.SMEM), vmem, hbm, hbm, hbm, hbm, hbm,
            ],
            out_specs=vmem,
            scratch_shapes=scratch,
            compiler_params=pltpu.CompilerParams(
                collective_id=0, has_side_effects=True, vmem_limit_bytes=56 << 20
            ),
        )(features, tile_mask, tile_cols.T, replicas, degree.reshape(1, masters), s1, n1, s2, n2)

    return jax.shard_map(
        on_device,
        mesh=mesh,
        in_specs=(
            P("feat", "dom"),
            P("dom", None, None, None),
            P("dom", None),
            P(None, "dom"),
            P("dom"),
            P(),
            P(),
            P(),
            P(),
        ),
        out_specs=P("feat", "dom"),
        check_vma=False,
    )
```

```python
import jax
import jax.numpy as jnp
from jax import lax
from jax.experimental import pallas as pl
from jax.experimental.pallas import tpu as pltpu
from jax.sharding import PartitionSpec as P

F32, BF16, I32 = jnp.float32, jnp.bfloat16, jnp.int32
MESH = pl.DeviceIdType.MESH
LANES = 128
TO1, BACK1, TO2, BACK2 = 2, 2, 2, 4
UNROLL_TAKE, UNROLL_SERVE, UNROLL_OPEN, UNROLL_AGG, UNROLL_COMB = 4, 4, 8, 8, 8
LO = 256
NN = (((1,), (0,)), ((), ()))
NT = (((1,), (1,)), ((), ()))


def loop(first, last, unroll, body):
    def some(i, _):
        for u in range(unroll):
            body(first + i * unroll + u)
        return 0

    lax.fori_loop(0, (last - first) // unroll, some, 0)


def dot(a, b, dims=NN):
    return lax.dot_general(a, b, dims, preferred_element_type=F32)


def kernel(
    doms, feats, cap,
    feat_hbm, mask_ref, cols_ref, reps_ref, deg_hbm, s1_hbm, n1_hbm, s2_hbm, n2_hbm,
    out_ref,
    feat_ref, deg_ref, s1_ref, n1_ref, s2_ref, n2_ref,
    stage, adj, gate_a, pick_a, gate_b, pick_b, pick_bt, want_out, want_in, whi,
    w1s, w1n, w2s, w2n, stacked, unfolded, local, own1, own2, mirror_part,
    total, plain, hid, agg1, agg2, feat_all, hid_all, agg1_all, agg2_all,
    box_f1, box_r1, box_f2, box_r2, got_f1, got_r1, got_f2, got_r2,
    in_sem, mask_sem, send_sem, recv_sem, feat_send, feat_recv,
):
    me, part = lax.axis_index("dom"), lax.axis_index("feat")
    per_row, blocks = cols_ref.shape
    tile = mask_ref.shape[-1]
    masters, mirrors = feat_ref.shape[1], reps_ref.shape[1]
    groups = doms * cap // LO
    each = LO // cap
    quarters = masters // LO
    master_blocks = masters // tile
    low = lax.broadcasted_iota(I32, (1, LANES), 1) < cap

    barrier = pltpu.get_barrier_semaphore()

    def greet(d, _):
        pl.semaphore_signal(
            barrier, 1, device_id={"dom": lax.rem(me + d, doms)}, device_id_type=MESH
        )
        return 0

    lax.fori_loop(1, doms, greet, 0)
    for d in range(1, feats):
        pl.semaphore_signal(
            barrier, 1, device_id={"feat": lax.rem(part + d, feats)}, device_id_type=MESH
        )

    inputs = [
        pltpu.make_async_copy(source, target, in_sem.at[i])
        for i, (source, target) in enumerate(
            (
                (feat_hbm, feat_ref), (s1_hbm, s1_ref), (n1_hbm, n1_ref),
                (s2_hbm, s2_ref), (n2_hbm, n2_ref), (deg_hbm, deg_ref),
            )
        )
    ]
    for copy in inputs:
        copy.start()
    for i in range(blocks):
        pltpu.make_async_copy(mask_ref.at[i], stage.at[i], mask_sem.at[i]).start()

    position = reps_ref[0:1, :] * cap + reps_ref[1:2, :]
    slot_group, slot_column = position >> 8, position & (LO - 1)
    for j in range(0, mirrors, LO):
        rows = lax.broadcasted_iota(I32, (LO, LO), 0)
        hit = rows == slot_column[:, j : j + LO]
        pick_b[:, j : j + LO] = jnp.where(hit, 1.0, 0.0).astype(BF16)
    row = reps_ref[2:3, :]
    here = lax.broadcasted_iota(I32, (groups, mirrors), 0) == slot_group
    tails = jnp.where(here, row & (LO - 1), 0)
    heads = jnp.where(here, (row >> 8) + 1, 0)
    words = jnp.concatenate([tails, heads], axis=0).astype(F32).astype(BF16)
    slots = dot(words, pick_b[...], NT)
    slots = slots[groups:] * float(LO) + slots[:groups]
    for c in range(LO // LANES):
        pair = slots[:, c * LANES : (c + 1) * LANES]
        even = jnp.where(low, pair, 0.0)
        odd = jnp.where(low, pltpu.roll(pair, cap, 1), 0.0)
        for h in range(groups):
            want_out[each * h + 2 * c] = even[h : h + 1]
            want_out[each * h + 2 * c + 1] = odd[h : h + 1]
    want_in[me] = jnp.zeros((1, LANES), F32)

    pl.semaphore_wait(barrier, doms - 1 + feats - 1)

    def send(box, got, which, q):
        @pl.when(q != me)
        def _():
            pltpu.make_async_remote_copy(
                src_ref=box.at[q],
                dst_ref=got.at[me],
                send_sem=send_sem.at[which],
                recv_sem=recv_sem.at[which],
                device_id={"dom": q},
                device_id_type=MESH,
            ).start()

    def arrived(got, which):
        rest = got.at[pl.ds(0, doms - 1)]
        pltpu.make_async_copy(rest, rest, recv_sem.at[which]).wait()

    def sent(box, which):
        rest = box.at[pl.ds(0, doms - 1)]
        pltpu.make_async_copy(rest, rest, send_sem.at[which]).wait()

    def share(mine, everyone, which):
        everyone[part] = mine[...]
        for d in range(1, feats):
            pltpu.make_async_remote_copy(
                src_ref=mine,
                dst_ref=everyone.at[part],
                send_sem=feat_send.at[which],
                recv_sem=feat_recv.at[which],
                device_id={"feat": lax.rem(part + d, feats)},
                device_id_type=MESH,
            ).start()

    def shared(everyone, which):
        rest = everyone.at[pl.ds(0, feats - 1)]
        pltpu.make_async_copy(rest, rest, feat_recv.at[which]).wait()

    def all_sent(everyone, which):
        rest = everyone.at[pl.ds(0, feats - 1)]
        pltpu.make_async_copy(rest, rest, feat_send.at[which]).wait()

    def ask(d, _):
        send(want_out, want_in, 0, lax.rem(me + d, doms))
        return 0

    lax.fori_loop(1, doms, ask, 0)
    for copy in inputs:
        copy.wait()
    share(feat_ref, feat_all, 0)

    width = w1s.shape[0]
    column = lax.broadcasted_iota(I32, (width, s1_ref.shape[1]), 1)
    wanted = lax.broadcasted_iota(I32, column.shape, 0) + part * width
    choose = jnp.where(column == wanted, 1.0, 0.0).astype(BF16)
    w1s[...] = dot(choose, s1_ref[...], NT).astype(BF16)
    w2s[...] = dot(choose, s2_ref[...], NT).astype(BF16)
    for source, target in ((n1_ref, w1n), (n2_ref, w2n)):
        mine = source.shape[0] // feats
        for a in range(target.shape[0]):
            n = mine // target.shape[0]
            rows = [source[f * mine + a * n : f * mine + (a + 1) * n] for f in range(feats)]
            target[a] = dot(choose, jnp.concatenate(rows, axis=0), NT).astype(BF16)

    for h in range(groups):
        hit = jnp.where(slot_group == h, 1.0, 0.0)
        gate_b[h] = jnp.broadcast_to(hit, (16, mirrors)).astype(BF16)

    for j in range(0, mirrors, LO):
        pick_bt[j : j + LO] = jnp.transpose(pick_b[:, j : j + LO].astype(F32)).astype(BF16)

    arrived(want_in, 0)

    def read_wants(g):
        parts = []
        for c in range(LO // LANES):
            even = want_in[each * g + 2 * c]
            odd = pltpu.roll(want_in[each * g + 2 * c + 1], cap, 1)
            parts.append(jnp.where(low, even, odd))
        value = jnp.concatenate(parts, axis=1).astype(I32)
        hit = lax.broadcasted_iota(I32, (LO, LO), 0) == (value & (LO - 1))
        pick_a[g] = jnp.where(hit, 1.0, 0.0).astype(BF16)
        quarter = value >> 8
        whi[g] = quarter
        for h in range(quarters):
            mine = jnp.where(quarter == h + 1, 1.0, 0.0)
            gate_a[g, h] = jnp.broadcast_to(mine, (16, LO)).astype(BF16)


    def fold(values, box, g, n):
        half = n // 2
        for c in range(LO // LANES):
            pair = values[:, c * LANES : (c + 1) * LANES]
            top, bottom = pair[:half], pltpu.roll(pair[half:], cap, 1)
            even = jnp.where(low, top, bottom)
            odd = pltpu.roll(jnp.where(low, bottom, top), cap, 1)
            box[each * g + 2 * c] = even.astype(BF16)
            box[each * g + 2 * c + 1] = odd.astype(BF16)

    def send_group(box, got, which, g):
        for i in range(each):
            send(box, got, which, each * g + lax.rem(me + i, each))

    def unfold(got, g):
        tops, bottoms = [], []
        for c in range(LO // LANES):
            even = got[each * g + 2 * c].astype(F32)
            odd = pltpu.roll(got[each * g + 2 * c + 1].astype(F32), cap, 1)
            tops.append(jnp.where(low, even, odd))
            bottoms.append(pltpu.roll(jnp.where(low, odd, even), cap, 1))
        top, bottom = jnp.concatenate(tops, axis=1), jnp.concatenate(bottoms, axis=1)
        return jnp.concatenate([top, bottom], axis=0).astype(BF16)

    def serve(values, n, box, got, which, first=False):
        got[me] = jnp.zeros((n // 2, LANES), BF16)
        for h in range(quarters):
            stacked[pl.ds(h * n, n), :] = values[:, h * LO : (h + 1) * LO]

        rows = stacked[pl.ds(0, quarters * n), :]

        def some(d, _):
            these = [lax.rem(me // each + d * UNROLL_SERVE + u, groups) for u in range(UNROLL_SERVE)]
            if first:
                for g in these:
                    read_wants(g)
            found = [dot(rows, pick_a[g]) for g in these]
            for g, f in zip(these, found):
                quarter = whi[g]
                answer = jnp.zeros((n, LO), F32)
                for h in range(quarters):
                    answer = jnp.where(quarter == h + 1, f[h * n : (h + 1) * n], answer)
                fold(answer, box, g, n)
            for g in these:
                send_group(box, got, which, g)
            return 0

        lax.fori_loop(0, groups // UNROLL_SERVE, some, 0)

    def place(values, got, which, n):
        for b in range(master_blocks):
            local[b, pl.ds(0, n), :] = values[:, b * tile : (b + 1) * tile]
        arrived(got, which)

        def open_up(g):
            unfolded[pl.ds(pl.multiple_of(g * n, n), n), :] = unfold(got, g)

        loop(0, groups, UNROLL_OPEN, open_up)
        for j in range(mirrors // LO):
            column = pick_b[:, j * LO : (j + 1) * LO]
            group = slot_group[:, j * LO : (j + 1) * LO]
            found = dot(unfolded[pl.ds(0, groups * n), :], column)
            answer = jnp.zeros((n, LO), F32)
            for h in range(groups):
                answer = jnp.where(group == h, found[h * n : (h + 1) * n], answer)
            answer = answer.astype(BF16)
            for c in range(LO // tile):
                b = master_blocks + j * (LO // tile) + c
                local[b, pl.ds(0, n), :] = answer[:, c * tile : (c + 1) * tile]

    def aggregate(n, own):
        def row_block(i):
            sources = [local[cols_ref[k, i], pl.ds(0, n), :] for k in range(per_row)]
            return dot(jnp.concatenate(sources, axis=1), adj[i])

        def of_masters(d, _):
            these = [d * UNROLL_AGG + u for u in range(UNROLL_AGG)]
            for i, sums in [(i, row_block(i)) for i in these]:
                own[i] = sums
            return 0

        def of_mirrors(d, _):
            these = [d * UNROLL_AGG + u for u in range(UNROLL_AGG)]
            for i, sums in [(i, row_block(i + master_blocks)) for i in these]:
                mirror_part[i, pl.ds(0, n), :] = sums.astype(BF16)
            return 0

        if own is None:
            lax.fori_loop(0, (blocks - master_blocks) // UNROLL_AGG, of_mirrors, 0)
        else:
            lax.fori_loop(0, master_blocks // UNROLL_AGG, of_masters, 0)

    def give_back(n, at, box, got, which):
        got[me] = jnp.zeros((n // 2, LANES), BF16)
        step = min(groups, LO // 2 // n)
        sums = jnp.concatenate(
            [mirror_part[b, pl.ds(at, n), :] for b in range(mirrors // tile)], axis=1
        )

        def some(d, _):
            first = lax.rem(me // each // step + d, groups // step) * step
            rows = []
            for h in range(step):
                gate = gate_b[first + h]
                rows.append(sums * jnp.concatenate([gate] * (n // 16), axis=0))
            slots = dot(jnp.concatenate(rows, axis=0), pick_bt[...])
            for h in range(step):
                fold(slots[h * n : (h + 1) * n], box, first + h, n)
            for h in range(step):
                send_group(box, got, which, first + h)
            return 0

        lax.fori_loop(0, groups // step, some, 0)

    def combine(n, own, at, got, which, mean):
        arrived(got, which)
        size = quarters * n
        total[pl.ds(0, size), :] = jnp.zeros((size, LO), F32)

        def some(d, _):
            sums = []
            for g in [d * UNROLL_COMB + u for u in range(UNROLL_COMB)]:
                values = unfold(got, g)
                rows = []
                for h in range(quarters):
                    gate = gate_a[g, h]
                    rows.append(values * jnp.concatenate([gate] * (n // 16), axis=0))
                sums.append(dot(jnp.concatenate(rows, axis=0), pick_a[g], NT))
            total[pl.ds(0, size), :] += sum(sums[1:], sums[0])
            return 0

        lax.fori_loop(0, groups // UNROLL_COMB, some, 0)
        for b in range(master_blocks):
            h, c = divmod(b * tile, LO)
            sums = own[b, pl.ds(at, n), :] + total[pl.ds(h * n, n), c : c + tile]
            scale = deg_ref[:, b * tile : (b + 1) * tile].astype(F32)
            mean[:, b * tile : (b + 1) * tile] = (sums / scale).astype(BF16)

    def mix_own(weights, inputs, which):
        shared(inputs, which)
        count = inputs.shape[0] * inputs.shape[1]
        plain[...] = dot(weights[...], inputs[...].reshape(count, masters))

    def mix_mean(weights, means, first, n):
        result = plain[first : first + n]
        for a in range(weights.shape[0]):
            count = means.shape[1] * means.shape[2]
            result += dot(weights[a, first : first + n, :], means[a].reshape(count, masters))
        return result

    def layer(values, weights, inputs, which_in, own, mean, means, which, to, back, first_share):
        count, n = to[1].shape[0], 2 * to[1].shape[2]
        count_back, n_back = mean.shape[:2]
        for a in range(count):
            place(values[a * n : (a + 1) * n], to[1].at[a], which + a, n)
            aggregate(n, None)
            for at in range(0, n, n_back):
                b = (a * n + at) // n_back
                give_back(n_back, at, back[0].at[b], back[1].at[b], which + count + b)
            aggregate(n, own.at[a])
        mix_own(weights, inputs, which_in)
        for b in range(count_back):
            a, at = divmod(b * n_back, n)
            combine(n_back, own.at[a], at, back[1].at[b], which + count + b, mean.at[b])
            share(mean.at[b], means.at[b], first_share + b)
        for b in range(count_back):
            shared(means.at[b], first_share + b)

    to1, n1 = box_f1.shape[0], 2 * box_f1.shape[2]
    to2, n2 = box_f2.shape[0], 2 * box_f2.shape[2]
    base2, share2 = 1 + to1 + agg1.shape[0], 2 + agg1.shape[0]
    boxes1, boxes2 = (box_f1, got_f1), (box_f2, got_f2)
    back1, back2 = (box_r1, got_r1), (box_r2, got_r2)
    for a in range(to1):
        values = feat_ref[a * n1 : (a + 1) * n1]
        serve(values, n1, box_f1.at[a], got_f1.at[a], 1 + a, a == 0)

    def take_block(i):
        pltpu.make_async_copy(mask_ref.at[i], stage.at[i], mask_sem.at[i]).wait()
        for k in range(per_row):
            entries = stage[i, k].astype(F32)
            adj[i, k * tile : (k + 1) * tile, :] = jnp.transpose(entries).astype(BF16)

    loop(0, blocks, UNROLL_TAKE, take_block)
    layer(feat_ref, w1s, feat_all, 0, own1, agg1, agg1_all, 1, boxes1, back1, 2)
    for a in range(to2):
        rows = jnp.maximum(mix_mean(w1n, agg1_all, a * n2, n2), 0.0).astype(BF16)
        hid[a * n2 : (a + 1) * n2] = rows
        serve(hid[a * n2 : (a + 1) * n2], n2, box_f2.at[a], got_f2.at[a], base2 + a)
    share(hid, hid_all, 1)
    layer(hid, w2s, hid_all, 1, own2, agg2, agg2_all, base2, boxes2, back2, share2)
    out_ref[...] = mix_mean(w2n, agg2_all, 0, width).astype(BF16)

    sent(want_out, 0)
    which = 1
    for box in (box_f1, box_r1, box_f2, box_r2):
        for a in range(box.shape[0]):
            sent(box.at[a], which)
            which += 1
    all_sent(feat_all, 0)
    all_sent(hid_all, 1)
    which = 2
    for means in (agg1_all, agg2_all):
        for a in range(means.shape[0]):
            all_sent(means.at[a], which)
            which += 1


def solution(mesh):
    doms, feats = mesh.shape["dom"], mesh.shape["feat"]

    def on_device(features, tile_mask, tile_cols, replicas, degree, s1, n1, s2, n2):
        rows, masters = features.shape
        mirrors = replicas.shape[1]
        cap = 2 * mirrors // doms
        blocks, per_row, tile, _ = tile_mask.shape
        wide = s1.shape[1] // feats
        groups, quarters = doms * cap // LO, masters // LO
        t1, t2, b1, b2 = rows // TO1, wide // TO2, rows // BACK1, wide // BACK2
        most = max(t1, t2)
        vmem = pl.BlockSpec(memory_space=pltpu.VMEM)
        hbm = pl.BlockSpec(memory_space=pl.ANY)
        boxes = [
            pltpu.VMEM((count, doms, n // 2, LANES), BF16)
            for count, n in ((TO1, t1), (BACK1, b1), (TO2, t2), (BACK2, b2))
        ]
        dma = pltpu.SemaphoreType.DMA
        exchanges, shares = 1 + TO1 + BACK1 + TO2 + BACK2, 2 + BACK1 + BACK2
        scratch = [
            pltpu.VMEM(features.shape, BF16),
            pltpu.VMEM((1, masters), I32),
            *(pltpu.VMEM(w.shape, BF16) for w in (s1, n1, s2, n2)),
            pltpu.VMEM((blocks, per_row, tile, tile), I32),
            pltpu.VMEM((blocks, per_row * tile, tile), BF16),
            pltpu.VMEM((groups, quarters, 16, LO), BF16),
            pltpu.VMEM((groups, LO, LO), BF16),
            pltpu.VMEM((groups, 16, mirrors), BF16),
            pltpu.VMEM((LO, mirrors), BF16),
            pltpu.VMEM((mirrors, LO), BF16),
            pltpu.VMEM((doms, 1, LANES), F32),
            pltpu.VMEM((doms, 1, LANES), F32),
            pltpu.VMEM((groups, 1, LO), I32),
            pltpu.VMEM((wide, s1.shape[0]), BF16),
            pltpu.VMEM((BACK1, wide, n1.shape[0] // BACK1), BF16),
            pltpu.VMEM((wide, s2.shape[0]), BF16),
            pltpu.VMEM((BACK2, wide, n2.shape[0] // BACK2), BF16),
            pltpu.VMEM((quarters * most, LO), BF16),
            pltpu.VMEM((groups * most, LO), BF16),
            pltpu.VMEM((blocks, most, tile), BF16),
            pltpu.VMEM((TO1, masters // tile, t1, tile), F32),
            pltpu.VMEM((TO2, masters // tile, t2, tile), F32),
            pltpu.VMEM((mirrors // tile, most, tile), BF16),
            pltpu.VMEM((quarters * most, LO), F32),
            pltpu.VMEM((wide, masters), F32),
            pltpu.VMEM((wide, masters), BF16),
            pltpu.VMEM((BACK1, b1, masters), BF16),
            pltpu.VMEM((BACK2, b2, masters), BF16),
            pltpu.VMEM((feats, rows, masters), BF16),
            pltpu.VMEM((feats, wide, masters), BF16),
            pltpu.VMEM((BACK1, feats, b1, masters), BF16),
            pltpu.VMEM((BACK2, feats, b2, masters), BF16),
            *boxes, *boxes,
            dma((6,)), dma((blocks,)), dma((exchanges,)), dma((exchanges,)),
            dma((shares,)), dma((shares,)),
        ]
        return pl.pallas_call(
            lambda *refs: kernel(doms, feats, cap, *refs),
            name="two_layers",
            out_shape=jax.ShapeDtypeStruct((wide, masters), BF16),
            in_specs=[
                hbm, hbm, pl.BlockSpec(memory_space=pltpu.SMEM), vmem, hbm, hbm, hbm, hbm, hbm,
            ],
            out_specs=vmem,
            scratch_shapes=scratch,
            compiler_params=pltpu.CompilerParams(
                collective_id=0, has_side_effects=True, vmem_limit_bytes=56 << 20
            ),
        )(features, tile_mask, tile_cols.T, replicas, degree.reshape(1, masters), s1, n1, s2, n2)

    return jax.shard_map(
        on_device,
        mesh=mesh,
        in_specs=(
            P("feat", "dom"),
            P("dom", None, None, None),
            P("dom", None),
            P(None, "dom"),
            P("dom"),
            P(),
            P(),
            P(),
            P(),
        ),
        out_specs=P("feat", "dom"),
        check_vma=False,
    )
```

```python
import jax
import jax.numpy as jnp
from jax import lax
from jax.experimental import pallas as pl
from jax.experimental.pallas import tpu as pltpu
from jax.sharding import PartitionSpec as P

F32, BF16, I32 = jnp.float32, jnp.bfloat16, jnp.int32
MESH = pl.DeviceIdType.MESH
LANES = 128
TO1, BACK1, TO2, BACK2 = 2, 2, 2, 4
UNROLL_TAKE, UNROLL_SERVE, UNROLL_OPEN, UNROLL_AGG, UNROLL_COMB = 4, 4, 8, 8, 8
LO = 256
NN = (((1,), (0,)), ((), ()))
NT = (((1,), (1,)), ((), ()))


def loop(first, last, unroll, body):
    def some(i, _):
        for u in range(unroll):
            body(first + i * unroll + u)
        return 0

    lax.fori_loop(0, (last - first) // unroll, some, 0)


def dot(a, b, dims=NN):
    return lax.dot_general(a, b, dims, preferred_element_type=F32)


def kernel(
    doms, feats, cap,
    feat_hbm, mask_ref, cols_ref, reps_ref, deg_hbm, s1_hbm, n1_hbm, s2_hbm, n2_hbm,
    out_ref,
    feat_ref, deg_ref, s1_ref, n1_ref, s2_ref, n2_ref,
    stage, adj, gate_a, pick_a, gate_b, pick_b, pick_bt, want_out, want_in, whi,
    w1s, w1n, w2s, w2n, stacked, unfolded, local, own1, own2, mirror_part,
    total, plain, hid, agg1, agg2, feat_all, hid_all, agg1_all, agg2_all,
    box_f1, box_r1, box_f2, box_r2, got_f1, got_r1, got_f2, got_r2,
    in_sem, mask_sem, send_sem, recv_sem, feat_send, feat_recv,
):
    me, part = lax.axis_index("dom"), lax.axis_index("feat")
    per_row, blocks = cols_ref.shape
    tile = mask_ref.shape[-1]
    masters, mirrors = feat_ref.shape[1], reps_ref.shape[1]
    groups = doms * cap // LO
    each = LO // cap
    quarters = masters // LO
    master_blocks = masters // tile
    low = lax.broadcasted_iota(I32, (1, LANES), 1) < cap

    barrier = pltpu.get_barrier_semaphore()

    def greet(d, _):
        pl.semaphore_signal(
            barrier, 1, device_id={"dom": lax.rem(me + d, doms)}, device_id_type=MESH
        )
        return 0

    lax.fori_loop(1, doms, greet, 0)
    for d in range(1, feats):
        pl.semaphore_signal(
            barrier, 1, device_id={"feat": lax.rem(part + d, feats)}, device_id_type=MESH
        )

    inputs = [
        pltpu.make_async_copy(source, target, in_sem.at[i])
        for i, (source, target) in enumerate(
            (
                (feat_hbm, feat_ref), (s1_hbm, s1_ref), (n1_hbm, n1_ref),
                (s2_hbm, s2_ref), (n2_hbm, n2_ref), (deg_hbm, deg_ref),
            )
        )
    ]
    for copy in inputs:
        copy.start()

    position = reps_ref[0:1, :] * cap + reps_ref[1:2, :]
    slot_group, slot_column = position >> 8, position & (LO - 1)
    for j in range(0, mirrors, LO):
        rows = lax.broadcasted_iota(I32, (LO, LO), 0)
        hit = rows == slot_column[:, j : j + LO]
        pick_b[:, j : j + LO] = jnp.where(hit, 1.0, 0.0).astype(BF16)
    row = reps_ref[2:3, :]
    here = lax.broadcasted_iota(I32, (groups, mirrors), 0) == slot_group
    tails = jnp.where(here, row & (LO - 1), 0)
    heads = jnp.where(here, (row >> 8) + 1, 0)
    words = jnp.concatenate([tails, heads], axis=0).astype(F32).astype(BF16)
    slots = dot(words, pick_b[...], NT)
    slots = slots[groups:] * float(LO) + slots[:groups]
    for c in range(LO // LANES):
        pair = slots[:, c * LANES : (c + 1) * LANES]
        even = jnp.where(low, pair, 0.0)
        odd = jnp.where(low, pltpu.roll(pair, cap, 1), 0.0)
        for h in range(groups):
            want_out[each * h + 2 * c] = even[h : h + 1]
            want_out[each * h + 2 * c + 1] = odd[h : h + 1]
    want_in[me] = jnp.zeros((1, LANES), F32)

    pl.semaphore_wait(barrier, doms - 1 + feats - 1)

    def send(box, got, which, q):
        @pl.when(q != me)
        def _():
            pltpu.make_async_remote_copy(
                src_ref=box.at[q],
                dst_ref=got.at[me],
                send_sem=send_sem.at[which],
                recv_sem=recv_sem.at[which],
                device_id={"dom": q},
                device_id_type=MESH,
            ).start()

    def arrived(got, which):
        rest = got.at[pl.ds(0, doms - 1)]
        pltpu.make_async_copy(rest, rest, recv_sem.at[which]).wait()

    def sent(box, which):
        rest = box.at[pl.ds(0, doms - 1)]
        pltpu.make_async_copy(rest, rest, send_sem.at[which]).wait()

    def share(mine, everyone, which):
        everyone[part] = mine[...]
        for d in range(1, feats):
            pltpu.make_async_remote_copy(
                src_ref=mine,
                dst_ref=everyone.at[part],
                send_sem=feat_send.at[which],
                recv_sem=feat_recv.at[which],
                device_id={"feat": lax.rem(part + d, feats)},
                device_id_type=MESH,
            ).start()

    def shared(everyone, which):
        rest = everyone.at[pl.ds(0, feats - 1)]
        pltpu.make_async_copy(rest, rest, feat_recv.at[which]).wait()

    def all_sent(everyone, which):
        rest = everyone.at[pl.ds(0, feats - 1)]
        pltpu.make_async_copy(rest, rest, feat_send.at[which]).wait()

    def ask(d, _):
        send(want_out, want_in, 0, lax.rem(me + d, doms))
        return 0

    lax.fori_loop(1, doms, ask, 0)
    for i in range(blocks):
        pltpu.make_async_copy(mask_ref.at[i], stage.at[i], mask_sem.at[i]).start()
    for copy in inputs:
        copy.wait()
    share(feat_ref, feat_all, 0)

    width = w1s.shape[0]
    column = lax.broadcasted_iota(I32, (width, s1_ref.shape[1]), 1)
    wanted = lax.broadcasted_iota(I32, column.shape, 0) + part * width
    choose = jnp.where(column == wanted, 1.0, 0.0).astype(BF16)
    w1s[...] = dot(choose, s1_ref[...], NT).astype(BF16)
    w2s[...] = dot(choose, s2_ref[...], NT).astype(BF16)
    for source, target in ((n1_ref, w1n), (n2_ref, w2n)):
        mine = source.shape[0] // feats
        for a in range(target.shape[0]):
            n = mine // target.shape[0]
            rows = [source[f * mine + a * n : f * mine + (a + 1) * n] for f in range(feats)]
            target[a] = dot(choose, jnp.concatenate(rows, axis=0), NT).astype(BF16)

    for h in range(groups):
        hit = jnp.where(slot_group == h, 1.0, 0.0)
        gate_b[h] = jnp.broadcast_to(hit, (16, mirrors)).astype(BF16)

    for j in range(0, mirrors, LO):
        pick_bt[j : j + LO] = jnp.transpose(pick_b[:, j : j + LO].astype(F32)).astype(BF16)

    arrived(want_in, 0)

    def read_wants(g):
        parts = []
        for c in range(LO // LANES):
            even = want_in[each * g + 2 * c]
            odd = pltpu.roll(want_in[each * g + 2 * c + 1], cap, 1)
            parts.append(jnp.where(low, even, odd))
        value = jnp.concatenate(parts, axis=1).astype(I32)
        hit = lax.broadcasted_iota(I32, (LO, LO), 0) == (value & (LO - 1))
        pick_a[g] = jnp.where(hit, 1.0, 0.0).astype(BF16)
        quarter = value >> 8
        whi[g] = quarter
        for h in range(quarters):
            mine = jnp.where(quarter == h + 1, 1.0, 0.0)
            gate_a[g, h] = jnp.broadcast_to(mine, (16, LO)).astype(BF16)


    def fold(values, box, g, n):
        half = n // 2
        for c in range(LO // LANES):
            pair = values[:, c * LANES : (c + 1) * LANES]
            top, bottom = pair[:half], pltpu.roll(pair[half:], cap, 1)
            even = jnp.where(low, top, bottom)
            odd = pltpu.roll(jnp.where(low, bottom, top), cap, 1)
            box[each * g + 2 * c] = even.astype(BF16)
            box[each * g + 2 * c + 1] = odd.astype(BF16)

    def send_group(box, got, which, g):
        for i in range(each):
            send(box, got, which, each * g + lax.rem(me + i, each))

    def unfold(got, g):
        tops, bottoms = [], []
        for c in range(LO // LANES):
            even = got[each * g + 2 * c].astype(F32)
            odd = pltpu.roll(got[each * g + 2 * c + 1].astype(F32), cap, 1)
            tops.append(jnp.where(low, even, odd))
            bottoms.append(pltpu.roll(jnp.where(low, odd, even), cap, 1))
        top, bottom = jnp.concatenate(tops, axis=1), jnp.concatenate(bottoms, axis=1)
        return jnp.concatenate([top, bottom], axis=0).astype(BF16)

    def serve(values, n, box, got, which, first=False):
        got[me] = jnp.zeros((n // 2, LANES), BF16)
        for h in range(quarters):
            stacked[pl.ds(h * n, n), :] = values[:, h * LO : (h + 1) * LO]

        rows = stacked[pl.ds(0, quarters * n), :]

        def some(d, _):
            these = [lax.rem(me // each + d * UNROLL_SERVE + u, groups) for u in range(UNROLL_SERVE)]
            if first:
                for g in these:
                    read_wants(g)
            found = [dot(rows, pick_a[g]) for g in these]
            for g, f in zip(these, found):
                quarter = whi[g]
                answer = jnp.zeros((n, LO), F32)
                for h in range(quarters):
                    answer = jnp.where(quarter == h + 1, f[h * n : (h + 1) * n], answer)
                fold(answer, box, g, n)
            for g in these:
                send_group(box, got, which, g)
            return 0

        lax.fori_loop(0, groups // UNROLL_SERVE, some, 0)

    def place(values, got, which, n):
        for b in range(master_blocks):
            local[b, pl.ds(0, n), :] = values[:, b * tile : (b + 1) * tile]
        arrived(got, which)

        def open_up(g):
            unfolded[pl.ds(pl.multiple_of(g * n, n), n), :] = unfold(got, g)

        loop(0, groups, UNROLL_OPEN, open_up)
        for j in range(mirrors // LO):
            column = pick_b[:, j * LO : (j + 1) * LO]
            group = slot_group[:, j * LO : (j + 1) * LO]
            found = dot(unfolded[pl.ds(0, groups * n), :], column)
            answer = jnp.zeros((n, LO), F32)
            for h in range(groups):
                answer = jnp.where(group == h, found[h * n : (h + 1) * n], answer)
            answer = answer.astype(BF16)
            for c in range(LO // tile):
                b = master_blocks + j * (LO // tile) + c
                local[b, pl.ds(0, n), :] = answer[:, c * tile : (c + 1) * tile]

    def aggregate(n, own):
        def row_block(i):
            sources = [local[cols_ref[k, i], pl.ds(0, n), :] for k in range(per_row)]
            return dot(jnp.concatenate(sources, axis=1), adj[i])

        def of_masters(d, _):
            these = [d * UNROLL_AGG + u for u in range(UNROLL_AGG)]
            for i, sums in [(i, row_block(i)) for i in these]:
                own[i] = sums
            return 0

        def of_mirrors(d, _):
            these = [d * UNROLL_AGG + u for u in range(UNROLL_AGG)]
            for i, sums in [(i, row_block(i + master_blocks)) for i in these]:
                mirror_part[i, pl.ds(0, n), :] = sums.astype(BF16)
            return 0

        if own is None:
            lax.fori_loop(0, (blocks - master_blocks) // UNROLL_AGG, of_mirrors, 0)
        else:
            lax.fori_loop(0, master_blocks // UNROLL_AGG, of_masters, 0)

    def give_back(n, at, box, got, which):
        got[me] = jnp.zeros((n // 2, LANES), BF16)
        step = min(groups, LO // n)
        sums = jnp.concatenate(
            [mirror_part[b, pl.ds(at, n), :] for b in range(mirrors // tile)], axis=1
        )

        def some(d, _):
            first = lax.rem(me // each // step + d, groups // step) * step
            rows = []
            for h in range(step):
                gate = gate_b[first + h]
                rows.append(sums * jnp.concatenate([gate] * (n // 16), axis=0))
            slots = dot(jnp.concatenate(rows, axis=0), pick_bt[...])
            for h in range(step):
                fold(slots[h * n : (h + 1) * n], box, first + h, n)
            for h in range(step):
                send_group(box, got, which, first + h)
            return 0

        lax.fori_loop(0, groups // step, some, 0)

    def combine(n, own, at, got, which, mean):
        arrived(got, which)
        size = quarters * n
        total[pl.ds(0, size), :] = jnp.zeros((size, LO), F32)

        def some(d, _):
            sums = []
            for g in [d * UNROLL_COMB + u for u in range(UNROLL_COMB)]:
                values = unfold(got, g)
                rows = []
                for h in range(quarters):
                    gate = gate_a[g, h]
                    rows.append(values * jnp.concatenate([gate] * (n // 16), axis=0))
                sums.append(dot(jnp.concatenate(rows, axis=0), pick_a[g], NT))
            total[pl.ds(0, size), :] += sum(sums[1:], sums[0])
            return 0

        lax.fori_loop(0, groups // UNROLL_COMB, some, 0)
        for b in range(master_blocks):
            h, c = divmod(b * tile, LO)
            sums = own[b, pl.ds(at, n), :] + total[pl.ds(h * n, n), c : c + tile]
            scale = deg_ref[:, b * tile : (b + 1) * tile].astype(F32)
            mean[:, b * tile : (b + 1) * tile] = (sums / scale).astype(BF16)

    def mix_own(weights, inputs, which):
        shared(inputs, which)
        count = inputs.shape[0] * inputs.shape[1]
        plain[...] = dot(weights[...], inputs[...].reshape(count, masters))

    def mix_mean(weights, means, first, n):
        result = plain[first : first + n]
        for a in range(weights.shape[0]):
            count = means.shape[1] * means.shape[2]
            result += dot(weights[a, first : first + n, :], means[a].reshape(count, masters))
        return result

    def layer(values, weights, inputs, which_in, own, mean, means, which, to, back, first_share):
        count, n = to[1].shape[0], 2 * to[1].shape[2]
        count_back, n_back = mean.shape[:2]
        for a in range(count):
            place(values[a * n : (a + 1) * n], to[1].at[a], which + a, n)
            aggregate(n, None)
            for at in range(0, n, n_back):
                b = (a * n + at) // n_back
                give_back(n_back, at, back[0].at[b], back[1].at[b], which + count + b)
            aggregate(n, own.at[a])
        mix_own(weights, inputs, which_in)
        for b in range(count_back):
            a, at = divmod(b * n_back, n)
            combine(n_back, own.at[a], at, back[1].at[b], which + count + b, mean.at[b])
            share(mean.at[b], means.at[b], first_share + b)
        for b in range(count_back):
            shared(means.at[b], first_share + b)

    to1, n1 = box_f1.shape[0], 2 * box_f1.shape[2]
    to2, n2 = box_f2.shape[0], 2 * box_f2.shape[2]
    base2, share2 = 1 + to1 + agg1.shape[0], 2 + agg1.shape[0]
    boxes1, boxes2 = (box_f1, got_f1), (box_f2, got_f2)
    back1, back2 = (box_r1, got_r1), (box_r2, got_r2)
    for a in range(to1):
        values = feat_ref[a * n1 : (a + 1) * n1]
        serve(values, n1, box_f1.at[a], got_f1.at[a], 1 + a, a == 0)

    def take_block(i):
        pltpu.make_async_copy(mask_ref.at[i], stage.at[i], mask_sem.at[i]).wait()
        for k in range(per_row):
            entries = stage[i, k].astype(F32)
            adj[i, k * tile : (k + 1) * tile, :] = jnp.transpose(entries).astype(BF16)

    loop(0, blocks, UNROLL_TAKE, take_block)
    layer(feat_ref, w1s, feat_all, 0, own1, agg1, agg1_all, 1, boxes1, back1, 2)
    for a in range(to2):
        rows = jnp.maximum(mix_mean(w1n, agg1_all, a * n2, n2), 0.0).astype(BF16)
        hid[a * n2 : (a + 1) * n2] = rows
        serve(hid[a * n2 : (a + 1) * n2], n2, box_f2.at[a], got_f2.at[a], base2 + a)
    share(hid, hid_all, 1)
    layer(hid, w2s, hid_all, 1, own2, agg2, agg2_all, base2, boxes2, back2, share2)
    out_ref[...] = mix_mean(w2n, agg2_all, 0, width).astype(BF16)

    sent(want_out, 0)
    which = 1
    for box in (box_f1, box_r1, box_f2, box_r2):
        for a in range(box.shape[0]):
            sent(box.at[a], which)
            which += 1
    all_sent(feat_all, 0)
    all_sent(hid_all, 1)
    which = 2
    for means in (agg1_all, agg2_all):
        for a in range(means.shape[0]):
            all_sent(means.at[a], which)
            which += 1


def solution(mesh):
    doms, feats = mesh.shape["dom"], mesh.shape["feat"]

    def on_device(features, tile_mask, tile_cols, replicas, degree, s1, n1, s2, n2):
        rows, masters = features.shape
        mirrors = replicas.shape[1]
        cap = 2 * mirrors // doms
        blocks, per_row, tile, _ = tile_mask.shape
        wide = s1.shape[1] // feats
        groups, quarters = doms * cap // LO, masters // LO
        t1, t2, b1, b2 = rows // TO1, wide // TO2, rows // BACK1, wide // BACK2
        most = max(t1, t2)
        vmem = pl.BlockSpec(memory_space=pltpu.VMEM)
        hbm = pl.BlockSpec(memory_space=pl.ANY)
        boxes = [
            pltpu.VMEM((count, doms, n // 2, LANES), BF16)
            for count, n in ((TO1, t1), (BACK1, b1), (TO2, t2), (BACK2, b2))
        ]
        dma = pltpu.SemaphoreType.DMA
        exchanges, shares = 1 + TO1 + BACK1 + TO2 + BACK2, 2 + BACK1 + BACK2
        scratch = [
            pltpu.VMEM(features.shape, BF16),
            pltpu.VMEM((1, masters), I32),
            *(pltpu.VMEM(w.shape, BF16) for w in (s1, n1, s2, n2)),
            pltpu.VMEM((blocks, per_row, tile, tile), I32),
            pltpu.VMEM((blocks, per_row * tile, tile), BF16),
            pltpu.VMEM((groups, quarters, 16, LO), BF16),
            pltpu.VMEM((groups, LO, LO), BF16),
            pltpu.VMEM((groups, 16, mirrors), BF16),
            pltpu.VMEM((LO, mirrors), BF16),
            pltpu.VMEM((mirrors, LO), BF16),
            pltpu.VMEM((doms, 1, LANES), F32),
            pltpu.VMEM((doms, 1, LANES), F32),
            pltpu.VMEM((groups, 1, LO), I32),
            pltpu.VMEM((wide, s1.shape[0]), BF16),
            pltpu.VMEM((BACK1, wide, n1.shape[0] // BACK1), BF16),
            pltpu.VMEM((wide, s2.shape[0]), BF16),
            pltpu.VMEM((BACK2, wide, n2.shape[0] // BACK2), BF16),
            pltpu.VMEM((quarters * most, LO), BF16),
            pltpu.VMEM((groups * most, LO), BF16),
            pltpu.VMEM((blocks, most, tile), BF16),
            pltpu.VMEM((TO1, masters // tile, t1, tile), F32),
            pltpu.VMEM((TO2, masters // tile, t2, tile), F32),
            pltpu.VMEM((mirrors // tile, most, tile), BF16),
            pltpu.VMEM((quarters * most, LO), F32),
            pltpu.VMEM((wide, masters), F32),
            pltpu.VMEM((wide, masters), BF16),
            pltpu.VMEM((BACK1, b1, masters), BF16),
            pltpu.VMEM((BACK2, b2, masters), BF16),
            pltpu.VMEM((feats, rows, masters), BF16),
            pltpu.VMEM((feats, wide, masters), BF16),
            pltpu.VMEM((BACK1, feats, b1, masters), BF16),
            pltpu.VMEM((BACK2, feats, b2, masters), BF16),
            *boxes, *boxes,
            dma((6,)), dma((blocks,)), dma((exchanges,)), dma((exchanges,)),
            dma((shares,)), dma((shares,)),
        ]
        return pl.pallas_call(
            lambda *refs: kernel(doms, feats, cap, *refs),
            name="two_layers",
            out_shape=jax.ShapeDtypeStruct((wide, masters), BF16),
            in_specs=[
                hbm, hbm, pl.BlockSpec(memory_space=pltpu.SMEM), vmem, hbm, hbm, hbm, hbm, hbm,
            ],
            out_specs=vmem,
            scratch_shapes=scratch,
            compiler_params=pltpu.CompilerParams(
                collective_id=0, has_side_effects=True, vmem_limit_bytes=56 << 20
            ),
        )(features, tile_mask, tile_cols.T, replicas, degree.reshape(1, masters), s1, n1, s2, n2)

    return jax.shard_map(
        on_device,
        mesh=mesh,
        in_specs=(
            P("feat", "dom"),
            P("dom", None, None, None),
            P("dom", None),
            P(None, "dom"),
            P("dom"),
            P(),
            P(),
            P(),
            P(),
        ),
        out_specs=P("feat", "dom"),
        check_vma=False,
    )
```

```python
import jax
import jax.numpy as jnp
from jax import lax
from jax.experimental import pallas as pl
from jax.experimental.pallas import tpu as pltpu
from jax.sharding import PartitionSpec as P

F32, BF16, I32 = jnp.float32, jnp.bfloat16, jnp.int32
MESH = pl.DeviceIdType.MESH
LANES = 128
TO1, BACK1, TO2, BACK2 = 2, 2, 2, 4
UNROLL_TAKE, UNROLL_SERVE, UNROLL_OPEN, UNROLL_AGG, UNROLL_COMB = 4, 4, 8, 8, 8
LO = 256
NN = (((1,), (0,)), ((), ()))
NT = (((1,), (1,)), ((), ()))


def loop(first, last, unroll, body):
    def some(i, _):
        for u in range(unroll):
            body(first + i * unroll + u)
        return 0

    lax.fori_loop(0, (last - first) // unroll, some, 0)


def dot(a, b, dims=NN):
    return lax.dot_general(a, b, dims, preferred_element_type=F32)


def kernel(
    doms, feats, cap,
    feat_hbm, mask_ref, cols_ref, reps_ref, deg_hbm, s1_hbm, n1_hbm, s2_hbm, n2_hbm,
    out_ref,
    feat_ref, deg_ref, s1_ref, n1_ref, s2_ref, n2_ref,
    stage, adj, gate_a, pick_a, gate_b, pick_b, pick_bt, want_out, want_in, whi,
    w1s, w1n, w2s, w2n, stacked, unfolded, local, own1, own2, mirror_part,
    total, plain, hid, agg1, agg2, feat_all, hid_all, agg1_all, agg2_all,
    box_f1, box_r1, box_f2, box_r2, got_f1, got_r1, got_f2, got_r2,
    in_sem, mask_sem, send_sem, recv_sem, feat_send, feat_recv,
):
    me, part = lax.axis_index("dom"), lax.axis_index("feat")
    per_row, blocks = cols_ref.shape
    tile = mask_ref.shape[-1]
    masters, mirrors = feat_ref.shape[1], reps_ref.shape[1]
    groups = doms * cap // LO
    each = LO // cap
    quarters = masters // LO
    master_blocks = masters // tile
    low = lax.broadcasted_iota(I32, (1, LANES), 1) < cap

    barrier = pltpu.get_barrier_semaphore()

    def greet(d, _):
        pl.semaphore_signal(
            barrier, 1, device_id={"dom": lax.rem(me + d, doms)}, device_id_type=MESH
        )
        return 0

    lax.fori_loop(1, doms, greet, 0)
    for d in range(1, feats):
        pl.semaphore_signal(
            barrier, 1, device_id={"feat": lax.rem(part + d, feats)}, device_id_type=MESH
        )

    inputs = [
        pltpu.make_async_copy(source, target, in_sem.at[i])
        for i, (source, target) in enumerate(
            (
                (feat_hbm, feat_ref), (s1_hbm, s1_ref), (n1_hbm, n1_ref),
                (s2_hbm, s2_ref), (n2_hbm, n2_ref), (deg_hbm, deg_ref),
            )
        )
    ]
    inputs[0].start()

    position = reps_ref[0:1, :] * cap + reps_ref[1:2, :]
    slot_group, slot_column = position >> 8, position & (LO - 1)
    for j in range(0, mirrors, LO):
        rows = lax.broadcasted_iota(I32, (LO, LO), 0)
        hit = rows == slot_column[:, j : j + LO]
        pick_b[:, j : j + LO] = jnp.where(hit, 1.0, 0.0).astype(BF16)
    row = reps_ref[2:3, :]
    here = lax.broadcasted_iota(I32, (groups, mirrors), 0) == slot_group
    tails = jnp.where(here, row & (LO - 1), 0)
    heads = jnp.where(here, (row >> 8) + 1, 0)
    words = jnp.concatenate([tails, heads], axis=0).astype(F32).astype(BF16)
    slots = dot(words, pick_b[...], NT)
    slots = slots[groups:] * float(LO) + slots[:groups]
    for c in range(LO // LANES):
        pair = slots[:, c * LANES : (c + 1) * LANES]
        even = jnp.where(low, pair, 0.0)
        odd = jnp.where(low, pltpu.roll(pair, cap, 1), 0.0)
        for h in range(groups):
            want_out[each * h + 2 * c] = even[h : h + 1]
            want_out[each * h + 2 * c + 1] = odd[h : h + 1]
    want_in[me] = jnp.zeros((1, LANES), F32)

    pl.semaphore_wait(barrier, doms - 1 + feats - 1)

    def send(box, got, which, q):
        @pl.when(q != me)
        def _():
            pltpu.make_async_remote_copy(
                src_ref=box.at[q],
                dst_ref=got.at[me],
                send_sem=send_sem.at[which],
                recv_sem=recv_sem.at[which],
                device_id={"dom": q},
                device_id_type=MESH,
            ).start()

    def arrived(got, which):
        rest = got.at[pl.ds(0, doms - 1)]
        pltpu.make_async_copy(rest, rest, recv_sem.at[which]).wait()

    def sent(box, which):
        rest = box.at[pl.ds(0, doms - 1)]
        pltpu.make_async_copy(rest, rest, send_sem.at[which]).wait()

    def share(mine, everyone, which):
        everyone[part] = mine[...]
        for d in range(1, feats):
            pltpu.make_async_remote_copy(
                src_ref=mine,
                dst_ref=everyone.at[part],
                send_sem=feat_send.at[which],
                recv_sem=feat_recv.at[which],
                device_id={"feat": lax.rem(part + d, feats)},
                device_id_type=MESH,
            ).start()

    def shared(everyone, which):
        rest = everyone.at[pl.ds(0, feats - 1)]
        pltpu.make_async_copy(rest, rest, feat_recv.at[which]).wait()

    def all_sent(everyone, which):
        rest = everyone.at[pl.ds(0, feats - 1)]
        pltpu.make_async_copy(rest, rest, feat_send.at[which]).wait()

    def ask(d, _):
        send(want_out, want_in, 0, lax.rem(me + d, doms))
        return 0

    lax.fori_loop(1, doms, ask, 0)
    for copy in inputs[1:]:
        copy.start()
    for i in range(blocks):
        pltpu.make_async_copy(mask_ref.at[i], stage.at[i], mask_sem.at[i]).start()
    inputs[0].wait()
    share(feat_ref, feat_all, 0)
    for copy in inputs[1:]:
        copy.wait()

    width = w1s.shape[0]
    column = lax.broadcasted_iota(I32, (width, s1_ref.shape[1]), 1)
    wanted = lax.broadcasted_iota(I32, column.shape, 0) + part * width
    choose = jnp.where(column == wanted, 1.0, 0.0).astype(BF16)
    w1s[...] = dot(choose, s1_ref[...], NT).astype(BF16)
    w2s[...] = dot(choose, s2_ref[...], NT).astype(BF16)
    for source, target in ((n1_ref, w1n), (n2_ref, w2n)):
        mine = source.shape[0] // feats
        for a in range(target.shape[0]):
            n = mine // target.shape[0]
            rows = [source[f * mine + a * n : f * mine + (a + 1) * n] for f in range(feats)]
            target[a] = dot(choose, jnp.concatenate(rows, axis=0), NT).astype(BF16)

    for h in range(groups):
        hit = jnp.where(slot_group == h, 1.0, 0.0)
        gate_b[h] = jnp.broadcast_to(hit, (16, mirrors)).astype(BF16)

    for j in range(0, mirrors, LO):
        pick_bt[j : j + LO] = jnp.transpose(pick_b[:, j : j + LO].astype(F32)).astype(BF16)

    arrived(want_in, 0)

    def read_wants(g):
        parts = []
        for c in range(LO // LANES):
            even = want_in[each * g + 2 * c]
            odd = pltpu.roll(want_in[each * g + 2 * c + 1], cap, 1)
            parts.append(jnp.where(low, even, odd))
        value = jnp.concatenate(parts, axis=1).astype(I32)
        hit = lax.broadcasted_iota(I32, (LO, LO), 0) == (value & (LO - 1))
        pick_a[g] = jnp.where(hit, 1.0, 0.0).astype(BF16)
        quarter = value >> 8
        whi[g] = quarter
        for h in range(quarters):
            mine = jnp.where(quarter == h + 1, 1.0, 0.0)
            gate_a[g, h] = jnp.broadcast_to(mine, (16, LO)).astype(BF16)


    def fold(values, box, g, n):
        half = n // 2
        for c in range(LO // LANES):
            pair = values[:, c * LANES : (c + 1) * LANES]
            top, bottom = pair[:half], pltpu.roll(pair[half:], cap, 1)
            even = jnp.where(low, top, bottom)
            odd = pltpu.roll(jnp.where(low, bottom, top), cap, 1)
            box[each * g + 2 * c] = even.astype(BF16)
            box[each * g + 2 * c + 1] = odd.astype(BF16)

    def send_group(box, got, which, g):
        for i in range(each):
            send(box, got, which, each * g + lax.rem(me + i, each))

    def unfold(got, g):
        tops, bottoms = [], []
        for c in range(LO // LANES):
            even = got[each * g + 2 * c].astype(F32)
            odd = pltpu.roll(got[each * g + 2 * c + 1].astype(F32), cap, 1)
            tops.append(jnp.where(low, even, odd))
            bottoms.append(pltpu.roll(jnp.where(low, odd, even), cap, 1))
        top, bottom = jnp.concatenate(tops, axis=1), jnp.concatenate(bottoms, axis=1)
        return jnp.concatenate([top, bottom], axis=0).astype(BF16)

    def serve(values, n, box, got, which, first=False):
        got[me] = jnp.zeros((n // 2, LANES), BF16)
        for h in range(quarters):
            stacked[pl.ds(h * n, n), :] = values[:, h * LO : (h + 1) * LO]

        rows = stacked[pl.ds(0, quarters * n), :]

        def some(d, _):
            these = [lax.rem(me // each + d * UNROLL_SERVE + u, groups) for u in range(UNROLL_SERVE)]
            if first:
                for g in these:
                    read_wants(g)
            found = [dot(rows, pick_a[g]) for g in these]
            for g, f in zip(these, found):
                quarter = whi[g]
                answer = jnp.zeros((n, LO), F32)
                for h in range(quarters):
                    answer = jnp.where(quarter == h + 1, f[h * n : (h + 1) * n], answer)
                fold(answer, box, g, n)
            for g in these:
                send_group(box, got, which, g)
            return 0

        lax.fori_loop(0, groups // UNROLL_SERVE, some, 0)

    def place(values, got, which, n):
        for b in range(master_blocks):
            local[b, pl.ds(0, n), :] = values[:, b * tile : (b + 1) * tile]
        arrived(got, which)

        def open_up(g):
            unfolded[pl.ds(pl.multiple_of(g * n, n), n), :] = unfold(got, g)

        loop(0, groups, UNROLL_OPEN, open_up)
        for j in range(mirrors // LO):
            column = pick_b[:, j * LO : (j + 1) * LO]
            group = slot_group[:, j * LO : (j + 1) * LO]
            found = dot(unfolded[pl.ds(0, groups * n), :], column)
            answer = jnp.zeros((n, LO), F32)
            for h in range(groups):
                answer = jnp.where(group == h, found[h * n : (h + 1) * n], answer)
            answer = answer.astype(BF16)
            for c in range(LO // tile):
                b = master_blocks + j * (LO // tile) + c
                local[b, pl.ds(0, n), :] = answer[:, c * tile : (c + 1) * tile]

    def aggregate(n, own):
        def row_block(i):
            sources = [local[cols_ref[k, i], pl.ds(0, n), :] for k in range(per_row)]
            return dot(jnp.concatenate(sources, axis=1), adj[i])

        def of_masters(d, _):
            these = [d * UNROLL_AGG + u for u in range(UNROLL_AGG)]
            for i, sums in [(i, row_block(i)) for i in these]:
                own[i] = sums
            return 0

        def of_mirrors(d, _):
            these = [d * UNROLL_AGG + u for u in range(UNROLL_AGG)]
            for i, sums in [(i, row_block(i + master_blocks)) for i in these]:
                mirror_part[i, pl.ds(0, n), :] = sums.astype(BF16)
            return 0

        if own is None:
            lax.fori_loop(0, (blocks - master_blocks) // UNROLL_AGG, of_mirrors, 0)
        else:
            lax.fori_loop(0, master_blocks // UNROLL_AGG, of_masters, 0)

    def give_back(n, at, box, got, which):
        got[me] = jnp.zeros((n // 2, LANES), BF16)
        step = min(groups, LO // n)
        sums = jnp.concatenate(
            [mirror_part[b, pl.ds(at, n), :] for b in range(mirrors // tile)], axis=1
        )

        def some(d, _):
            first = lax.rem(me // each // step + d, groups // step) * step
            rows = []
            for h in range(step):
                gate = gate_b[first + h]
                rows.append(sums * jnp.concatenate([gate] * (n // 16), axis=0))
            slots = dot(jnp.concatenate(rows, axis=0), pick_bt[...])
            for h in range(step):
                fold(slots[h * n : (h + 1) * n], box, first + h, n)
            for h in range(step):
                send_group(box, got, which, first + h)
            return 0

        lax.fori_loop(0, groups // step, some, 0)

    def combine(n, own, at, got, which, mean):
        arrived(got, which)
        size = quarters * n
        total[pl.ds(0, size), :] = jnp.zeros((size, LO), F32)

        def some(d, _):
            sums = []
            for g in [d * UNROLL_COMB + u for u in range(UNROLL_COMB)]:
                values = unfold(got, g)
                rows = []
                for h in range(quarters):
                    gate = gate_a[g, h]
                    rows.append(values * jnp.concatenate([gate] * (n // 16), axis=0))
                sums.append(dot(jnp.concatenate(rows, axis=0), pick_a[g], NT))
            total[pl.ds(0, size), :] += sum(sums[1:], sums[0])
            return 0

        lax.fori_loop(0, groups // UNROLL_COMB, some, 0)
        for b in range(master_blocks):
            h, c = divmod(b * tile, LO)
            sums = own[b, pl.ds(at, n), :] + total[pl.ds(h * n, n), c : c + tile]
            scale = deg_ref[:, b * tile : (b + 1) * tile].astype(F32)
            mean[:, b * tile : (b + 1) * tile] = (sums / scale).astype(BF16)

    def mix_own(weights, inputs, which):
        shared(inputs, which)
        count = inputs.shape[0] * inputs.shape[1]
        plain[...] = dot(weights[...], inputs[...].reshape(count, masters))

    def mix_mean(weights, means, first, n):
        result = plain[first : first + n]
        for a in range(weights.shape[0]):
            count = means.shape[1] * means.shape[2]
            result += dot(weights[a, first : first + n, :], means[a].reshape(count, masters))
        return result

    def layer(values, weights, inputs, which_in, own, mean, means, which, to, back, first_share):
        count, n = to[1].shape[0], 2 * to[1].shape[2]
        count_back, n_back = mean.shape[:2]
        for a in range(count):
            place(values[a * n : (a + 1) * n], to[1].at[a], which + a, n)
            aggregate(n, None)
            for at in range(0, n, n_back):
                b = (a * n + at) // n_back
                give_back(n_back, at, back[0].at[b], back[1].at[b], which + count + b)
            aggregate(n, own.at[a])
        mix_own(weights, inputs, which_in)
        for b in range(count_back):
            a, at = divmod(b * n_back, n)
            combine(n_back, own.at[a], at, back[1].at[b], which + count + b, mean.at[b])
            share(mean.at[b], means.at[b], first_share + b)
        for b in range(count_back):
            shared(means.at[b], first_share + b)

    to1, n1 = box_f1.shape[0], 2 * box_f1.shape[2]
    to2, n2 = box_f2.shape[0], 2 * box_f2.shape[2]
    base2, share2 = 1 + to1 + agg1.shape[0], 2 + agg1.shape[0]
    boxes1, boxes2 = (box_f1, got_f1), (box_f2, got_f2)
    back1, back2 = (box_r1, got_r1), (box_r2, got_r2)
    for a in range(to1):
        values = feat_ref[a * n1 : (a + 1) * n1]
        serve(values, n1, box_f1.at[a], got_f1.at[a], 1 + a, a == 0)

    def take_block(i):
        pltpu.make_async_copy(mask_ref.at[i], stage.at[i], mask_sem.at[i]).wait()
        for k in range(per_row):
            entries = stage[i, k].astype(F32)
            adj[i, k * tile : (k + 1) * tile, :] = jnp.transpose(entries).astype(BF16)

    loop(0, blocks, UNROLL_TAKE, take_block)
    layer(feat_ref, w1s, feat_all, 0, own1, agg1, agg1_all, 1, boxes1, back1, 2)
    for a in range(to2):
        rows = jnp.maximum(mix_mean(w1n, agg1_all, a * n2, n2), 0.0).astype(BF16)
        hid[a * n2 : (a + 1) * n2] = rows
        serve(hid[a * n2 : (a + 1) * n2], n2, box_f2.at[a], got_f2.at[a], base2 + a)
    share(hid, hid_all, 1)
    layer(hid, w2s, hid_all, 1, own2, agg2, agg2_all, base2, boxes2, back2, share2)
    out_ref[...] = mix_mean(w2n, agg2_all, 0, width).astype(BF16)

    sent(want_out, 0)
    which = 1
    for box in (box_f1, box_r1, box_f2, box_r2):
        for a in range(box.shape[0]):
            sent(box.at[a], which)
            which += 1
    all_sent(feat_all, 0)
    all_sent(hid_all, 1)
    which = 2
    for means in (agg1_all, agg2_all):
        for a in range(means.shape[0]):
            all_sent(means.at[a], which)
            which += 1


def solution(mesh):
    doms, feats = mesh.shape["dom"], mesh.shape["feat"]

    def on_device(features, tile_mask, tile_cols, replicas, degree, s1, n1, s2, n2):
        rows, masters = features.shape
        mirrors = replicas.shape[1]
        cap = 2 * mirrors // doms
        blocks, per_row, tile, _ = tile_mask.shape
        wide = s1.shape[1] // feats
        groups, quarters = doms * cap // LO, masters // LO
        t1, t2, b1, b2 = rows // TO1, wide // TO2, rows // BACK1, wide // BACK2
        most = max(t1, t2)
        vmem = pl.BlockSpec(memory_space=pltpu.VMEM)
        hbm = pl.BlockSpec(memory_space=pl.ANY)
        boxes = [
            pltpu.VMEM((count, doms, n // 2, LANES), BF16)
            for count, n in ((TO1, t1), (BACK1, b1), (TO2, t2), (BACK2, b2))
        ]
        dma = pltpu.SemaphoreType.DMA
        exchanges, shares = 1 + TO1 + BACK1 + TO2 + BACK2, 2 + BACK1 + BACK2
        scratch = [
            pltpu.VMEM(features.shape, BF16),
            pltpu.VMEM((1, masters), I32),
            *(pltpu.VMEM(w.shape, BF16) for w in (s1, n1, s2, n2)),
            pltpu.VMEM((blocks, per_row, tile, tile), I32),
            pltpu.VMEM((blocks, per_row * tile, tile), BF16),
            pltpu.VMEM((groups, quarters, 16, LO), BF16),
            pltpu.VMEM((groups, LO, LO), BF16),
            pltpu.VMEM((groups, 16, mirrors), BF16),
            pltpu.VMEM((LO, mirrors), BF16),
            pltpu.VMEM((mirrors, LO), BF16),
            pltpu.VMEM((doms, 1, LANES), F32),
            pltpu.VMEM((doms, 1, LANES), F32),
            pltpu.VMEM((groups, 1, LO), I32),
            pltpu.VMEM((wide, s1.shape[0]), BF16),
            pltpu.VMEM((BACK1, wide, n1.shape[0] // BACK1), BF16),
            pltpu.VMEM((wide, s2.shape[0]), BF16),
            pltpu.VMEM((BACK2, wide, n2.shape[0] // BACK2), BF16),
            pltpu.VMEM((quarters * most, LO), BF16),
            pltpu.VMEM((groups * most, LO), BF16),
            pltpu.VMEM((blocks, most, tile), BF16),
            pltpu.VMEM((TO1, masters // tile, t1, tile), F32),
            pltpu.VMEM((TO2, masters // tile, t2, tile), F32),
            pltpu.VMEM((mirrors // tile, most, tile), BF16),
            pltpu.VMEM((quarters * most, LO), F32),
            pltpu.VMEM((wide, masters), F32),
            pltpu.VMEM((wide, masters), BF16),
            pltpu.VMEM((BACK1, b1, masters), BF16),
            pltpu.VMEM((BACK2, b2, masters), BF16),
            pltpu.VMEM((feats, rows, masters), BF16),
            pltpu.VMEM((feats, wide, masters), BF16),
            pltpu.VMEM((BACK1, feats, b1, masters), BF16),
            pltpu.VMEM((BACK2, feats, b2, masters), BF16),
            *boxes, *boxes,
            dma((6,)), dma((blocks,)), dma((exchanges,)), dma((exchanges,)),
            dma((shares,)), dma((shares,)),
        ]
        return pl.pallas_call(
            lambda *refs: kernel(doms, feats, cap, *refs),
            name="two_layers",
            out_shape=jax.ShapeDtypeStruct((wide, masters), BF16),
            in_specs=[
                hbm, hbm, pl.BlockSpec(memory_space=pltpu.SMEM), vmem, hbm, hbm, hbm, hbm, hbm,
            ],
            out_specs=vmem,
            scratch_shapes=scratch,
            compiler_params=pltpu.CompilerParams(
                collective_id=0, has_side_effects=True, vmem_limit_bytes=56 << 20
            ),
        )(features, tile_mask, tile_cols.T, replicas, degree.reshape(1, masters), s1, n1, s2, n2)

    return jax.shard_map(
        on_device,
        mesh=mesh,
        in_specs=(
            P("feat", "dom"),
            P("dom", None, None, None),
            P("dom", None),
            P(None, "dom"),
            P("dom"),
            P(),
            P(),
            P(),
            P(),
        ),
        out_specs=P("feat", "dom"),
        check_vma=False,
    )
```
